768 devices in a mesh: slab: 96 (over x, z, core), tile: 8 (over y).
Axes of the slice: x: 4, y: 8, z: 12, core: 2. Of those that a mesh axis runs over, the one named last changes fastest.
Arguments:
- particles: float32 [24576, 16, 128], P(('slab', 'tile')), may hold values from -6 to 6, as said below
- dest_slot: int32 [24576], P(('slab', 'tile')), may hold values from 0 to 63, as said below
- neighbours: int32 [49152, 4], P(('slab', 'tile')), may hold values from 0 to 191, as said below
- counts: int32 [49152], P(('slab', 'tile')), may hold values from 1 to 4, as said below
Outputs:
- updated: float32 [49152, 16, 128], P(('slab', 'tile'))
- derived: float32 [49152, 5, 128], P(('slab', 'tile'))
The draws below stay inside these ranges and needn't reach their ends.
Inputs may be any that keep to these rules, and one draw needn't show every extreme that they name: `dest_slot`: A bin on device (s, t) with value d goes to tile d // 8 of slab s. The values of one device are distinct, so at most 8 of its bins go to one owner; in every slab some owner receives 8 bins from every device of the slab. `neighbours`: entries index the 192 candidates of the slot's device: first the slab on the lower side (periodic), then the device's own slots, then the higher side. Entry 0 is the slot itself; the entries of a row are distinct. `counts`: every device has a slot that uses all 4 entries. `particles`: positions lie in 0 to 2, masses in 0.5 / 512 to 2 / 512, energies in 0.5 to 4, smoothing lengths in 0.6 to 1; velocities and carried quantities lie within -6 to 6.
All inputs are finite; a program needn't handle non-finite values.
Results may differ from the reference program's by a relative error of at most 0.0003.
Values sent between devices are 32-bit elements; how exact they have to be, the bound alone decides.
A program may use at most 32 MiB of HBM per device.

```python
import math
import jax
import jax.numpy as jnp
from jax import lax

PARTICLE_FLOATS = 16
BIN_PARTICLES = 128
B_DEV = 32
NEIGHBOUR_COUNT = 4
OUTBOX_CELL_CAP = 8
PLACES_PER_CHIP = 64
NBINS = 24576
SLOT_COUNT = 49152
N_SLAB = 96
N_TILE = 8


def draw_particles(key, part):
    keys = jax.random.split(key, 6)
    place = jax.random.uniform(keys[0], (NBINS, 3, BIN_PARTICLES), minval=0.0, maxval=2.0)
    speed = jnp.clip(0.3 * jax.random.normal(keys[1], (NBINS, 3, BIN_PARTICLES)), -6.0, 6.0)
    masses = jnp.exp(jax.random.uniform(keys[2], (NBINS, BIN_PARTICLES), minval=math.log(0.5), maxval=math.log(2.0))) / (NEIGHBOUR_COUNT * BIN_PARTICLES)
    energy = jnp.exp(jax.random.uniform(keys[3], (NBINS, BIN_PARTICLES), minval=math.log(0.5), maxval=math.log(4.0)))
    smooth = jax.random.uniform(keys[4], (NBINS, BIN_PARTICLES), minval=0.6, maxval=1.0)
    carried = jnp.clip(jax.random.normal(keys[5], (NBINS, PARTICLE_FLOATS - 9, BIN_PARTICLES)), -6.0, 6.0)
    joined = jnp.concatenate([place, speed, masses[:, None], energy[:, None], smooth[:, None], carried], axis=1)
    return joined.astype(jnp.float32)


def draw_dest_slot(key, part):
    keys = jax.random.split(jax.random.fold_in(key, 11), 2)
    busiest_cells = jax.random.randint(keys[0], (N_SLAB,), 0, N_TILE)
    place_position = jnp.arange(PLACES_PER_CHIP, dtype=jnp.int32)
    cell_ranking = jax.random.randint(keys[1], (N_SLAB, N_TILE, PLACES_PER_CHIP), 0, 2 ** 20)
    added_reward = jnp.where(place_position[None, None, :] // OUTBOX_CELL_CAP == busiest_cells[:, None, None], 2 ** 21, 0)
    overall_number = (cell_ranking + added_reward) * PLACES_PER_CHIP + place_position[None, None, :]
    picked = lax.top_k(overall_number, B_DEV)[1].astype(jnp.int32)
    return picked.reshape((NBINS,))


def draw_neighbours(key, part):
    kernel_width = 3 * PLACES_PER_CHIP
    column_index = jnp.arange(kernel_width, dtype=jnp.int32)
    cell_ranking = jax.random.randint(jax.random.fold_in(key, 23), (SLOT_COUNT, kernel_width), 0, 2 ** 20) * kernel_width + column_index[None, :]
    self_term = PLACES_PER_CHIP + jnp.arange(SLOT_COUNT, dtype=jnp.int32) % PLACES_PER_CHIP
    cell_ranking = jnp.where(column_index[None, :] == self_term[:, None], -1, cell_ranking)
    others = lax.top_k(cell_ranking, NEIGHBOUR_COUNT - 1)[1].astype(jnp.int32)
    return jnp.concatenate([self_term[:, None], others], axis=1)


def draw_counts(key, part):
    sampled_rows = jax.random.randint(jax.random.fold_in(key, 37), (SLOT_COUNT,), 1, NEIGHBOUR_COUNT + 1)
    particle_rows = jnp.arange(SLOT_COUNT, dtype=jnp.int32)
    return jnp.where(particle_rows % PLACES_PER_CHIP == 0, NEIGHBOUR_COUNT, sampled_rows).astype(jnp.int32)


def setup_inputs(seed: int = 0) -> dict:
    seeds = jax.random.split(jax.random.key(seed), 5)
    particles = draw_particles(jax.random.fold_in(seeds[4], 71), 0)
    dest_slot = draw_dest_slot(jax.random.fold_in(seeds[4], 71), 0)
    neighbours = draw_neighbours(jax.random.fold_in(seeds[4], 71), 0)
    counts = draw_counts(jax.random.fold_in(seeds[4], 71), 0)
    return dict(particles=particles, dest_slot=dest_slot, neighbours=neighbours, counts=counts)


ADIABATIC = 5.0 / 3.0
TIMESTEP = 0.5
KERNEL_NORM = 21.0 / (16.0 * math.pi)

def pair_terms(near_place, near_width, far_place, far_width):
    offset = near_place[:, :, None] - far_place[:, None, :]
    spacing = jnp.sqrt(lax.optimization_barrier(jnp.sum(offset * offset, axis=0)))
    blended = 0.5 * (near_width[:, None] + far_width[None, :])
    ratio = spacing / blended
    remain = jnp.maximum(1.0 - 0.5 * ratio, 0.0)
    scaled = KERNEL_NORM / (blended * blended * blended)
    cubed = remain * remain * remain
    weight = scaled * cubed * remain * (1.0 + 2.0 * ratio)
    slope = -5.0 * scaled / (blended * blended) * cubed
    return (weight, slope, offset)

def slot_density(self_place, self_width, chosen, entries, pool_place, pool_mass, pool_width):
    active = (jnp.arange(chosen.shape[0]) < entries).astype(jnp.float32)
    weight, slope, offset = jax.vmap(pair_terms, in_axes=(None, None, 0, 0))(self_place, self_width, pool_place[chosen], pool_width[chosen])
    return lax.optimization_barrier(jnp.sum(weight * (pool_mass[chosen] * active[:, None])[:, None, :], axis=(0, 2)))

def slot_force(self_place, self_width, self_speed, self_ratio, chosen, entries, pool_place, pool_mass, pool_width, pool_speed, pool_ratio):
    active = (jnp.arange(chosen.shape[0]) < entries).astype(jnp.float32)
    weight, slope, offset = jax.vmap(pair_terms, in_axes=(None, None, 0, 0))(self_place, self_width, pool_place[chosen], pool_width[chosen])
    factor = (pool_mass[chosen] * active[:, None])[:, None, :] * slope
    pairing = factor * (self_ratio[None, :, None] + pool_ratio[chosen][:, None, :])
    accel = -lax.optimization_barrier(jnp.sum(pairing[:, None] * offset, axis=(0, 3)))
    relative = self_speed[None, :, :, None] - pool_speed[chosen][:, :, None, :]
    closing = lax.optimization_barrier(jnp.sum(relative * offset, axis=1))
    heating = self_ratio * lax.optimization_barrier(jnp.sum(factor * closing, axis=(0, 2)))
    return jnp.concatenate([accel, heating[None]], axis=0)

def over_slots(worker, per_slot, shared):
    overall_number = per_slot[0].shape[0]
    blocks = tuple((member.reshape((overall_number // 8, 8) + member.shape[1:]) for member in per_slot))

    def run(block):
        return jax.vmap(lambda *single: worker(*single, *shared))(*block)
    result = lax.map(run, blocks)
    return result.reshape((overall_number,) + result.shape[2:])

def density_pass(self_place, self_width, chosen, entries, pool_place, pool_mass, pool_width):
    return over_slots(slot_density, (self_place, self_width, chosen, entries), (pool_place, pool_mass, pool_width))

def force_pass(self_place, self_width, self_speed, self_ratio, chosen, entries, pool_place, pool_mass, pool_width, pool_speed, pool_ratio):
    return over_slots(slot_force, (self_place, self_width, self_speed, self_ratio, chosen, entries), (pool_place, pool_mass, pool_width, pool_speed, pool_ratio))

def pressure_of(local_density, energy):
    return (ADIABATIC - 1.0) * local_density * energy

def final_state(particle_states, local_density, change_rates):
    present = (particle_states[:, 6] > 0).astype(jnp.float32)
    speed = particle_states[:, 3:6] + TIMESTEP * change_rates[:, 0:3]
    place = particle_states[:, 0:3] + TIMESTEP * speed
    heat = particle_states[:, 7:8] + TIMESTEP * change_rates[:, 3:4]
    updated = jnp.concatenate([place, speed, particle_states[:, 6:7], heat, particle_states[:, 8:]], axis=1) * present[:, None, :]
    derived = jnp.concatenate([local_density[:, None], change_rates], axis=1) * present[:, None, :]
    return (updated, derived)

def surround(field):
    return jnp.concatenate([jnp.roll(field, 1, axis=0), field, jnp.roll(field, -1, axis=0)], axis=2)

def reference(particles, dest_slot, neighbours, counts):
    device_total = N_SLAB * N_TILE
    source = jnp.arange(NBINS, dtype=jnp.int32) // B_DEV
    source_slab = source // N_TILE
    source_tile = source % N_TILE
    target_owner = (source_slab * N_TILE + dest_slot // OUTBOX_CELL_CAP) * PLACES_PER_CHIP + source_tile * OUTBOX_CELL_CAP + dest_slot % OUTBOX_CELL_CAP
    particle_states = jnp.zeros((SLOT_COUNT, PARTICLE_FLOATS, BIN_PARTICLES), jnp.float32).at[target_owner].set(particles)
    layout = (N_SLAB, N_TILE, PLACES_PER_CHIP)
    grid = particle_states.reshape(layout + (PARTICLE_FLOATS, BIN_PARTICLES))
    masses = grid[:, :, :, 6]
    present = masses > 0
    smooth = jnp.where(present, grid[:, :, :, 8], 1.0)
    energy = grid[:, :, :, 7]
    pool_place = surround(grid[:, :, :, 0:3]).reshape((device_total, 3 * PLACES_PER_CHIP, 3, BIN_PARTICLES))
    pool_mass = surround(masses).reshape((device_total, 3 * PLACES_PER_CHIP, BIN_PARTICLES))
    pool_width = surround(smooth).reshape((device_total, 3 * PLACES_PER_CHIP, BIN_PARTICLES))
    pool_speed = surround(grid[:, :, :, 3:6]).reshape((device_total, 3 * PLACES_PER_CHIP, 3, BIN_PARTICLES))
    chosen = neighbours.reshape((device_total, PLACES_PER_CHIP, NEIGHBOUR_COUNT))
    entries = counts.reshape((device_total, PLACES_PER_CHIP))
    self_place = grid[:, :, :, 0:3].reshape((device_total, PLACES_PER_CHIP, 3, BIN_PARTICLES))
    self_width = smooth.reshape((device_total, PLACES_PER_CHIP, BIN_PARTICLES))
    self_speed = grid[:, :, :, 3:6].reshape((device_total, PLACES_PER_CHIP, 3, BIN_PARTICLES))
    local_density = lax.map(lambda pieces: density_pass(*pieces), (self_place, self_width, chosen, entries, pool_place, pool_mass, pool_width))
    local_density = local_density.reshape(layout + (BIN_PARTICLES,))
    pressure = pressure_of(local_density, energy)
    self_ratio = (pressure / jnp.square(jnp.where(present, local_density, 1.0))).reshape((device_total, PLACES_PER_CHIP, BIN_PARTICLES))
    pool_ratio = surround(pressure) / jnp.square(jnp.where(surround(present), surround(local_density), 1.0))
    pool_ratio = pool_ratio.reshape((device_total, 3 * PLACES_PER_CHIP, BIN_PARTICLES))
    change_rates = lax.map(lambda pieces: force_pass(*pieces), (self_place, self_width, self_speed, self_ratio, chosen, entries, pool_place, pool_mass, pool_width, pool_speed, pool_ratio))
    return final_state(particle_states, local_density.reshape((SLOT_COUNT, BIN_PARTICLES)), change_rates.reshape((SLOT_COUNT, 4, BIN_PARTICLES)))
```

```python
import functools
import math

import jax
import jax.numpy as jnp
from jax import lax
from jax.experimental import pallas as pl
from jax.experimental.pallas import tpu as pltpu
from jax.sharding import PartitionSpec as P

ADIABATIC = 5.0 / 3.0
TIMESTEP = 0.5
KERNEL_NORM = 21.0 / (16.0 * math.pi)
W_SCALE = 40.0 * KERNEL_NORM
G_SCALE = -160.0 * KERNEL_NORM

FIELDS = 16
CELL = 8
LANES = 128
ROWS = 32
ORDER = (0, 1, 2, 6, 8, 3, 4, 5, 7, 9, 10, 11, 12, 13, 14, 15)
GROUPS = ((0, 5), (5, 9), (9, 16))
F32 = jnp.float32
BF16 = jnp.bfloat16
MESH = pl.DeviceIdType.MESH


def halves(x, count):
    parts = []
    for _ in range(count - 1):
        part = x.astype(BF16).astype(F32)
        parts.append(part)
        x = x - part
    parts.append(x.astype(BF16).astype(F32))
    return parts


def kernel(
    n_slab,
    n_tile,
    nbr,
    cnt,
    dest,
    particles,
    updated,
    derived,
    pbuf,
    outbox,
    pool1,
    pool2,
    carried,
    poolr,
    xs,
    self_rows,
    cand_d,
    cand_s,
    force_rows,
    slopes,
    rho,
    sums,
    masses,
    in_sem,
    a2a_send,
    a2a_recv,
    halo_send,
    halo_recv,
    r_send,
    r_recv,
):
    slots = n_tile * CELL
    bins = pbuf.shape[0] // FIELDS
    groups = slots // CELL
    slab = lax.axis_index("slab")
    tile = lax.axis_index("tile")
    up = lax.rem(slab + 1, n_slab)
    down = lax.rem(slab + n_slab - 1, n_slab)

    load = pltpu.make_async_copy(particles, pbuf, in_sem)
    load.start()

    barrier = pltpu.get_barrier_semaphore()
    for i in range(1, n_tile):
        peer = lax.rem(tile + i, n_tile)
        pl.semaphore_signal(barrier, inc=1, device_id=(slab, peer), device_id_type=MESH)
    for side in (up, down):
        pl.semaphore_signal(barrier, inc=1, device_id=(side, tile), device_id_type=MESH)

    zeros = jnp.zeros((CELL, LANES), F32)
    ones = jnp.ones((CELL, LANES), F32)

    @pl.loop(0, slots)
    def _(i):
        for r in (16, 24):
            self_rows[pl.ds(pl.multiple_of(i * ROWS + r, 8), CELL), :] = zeros

    @pl.loop(0, 3 * slots)
    def _(i):
        for r in (16, 24):
            cand_d[pl.ds(pl.multiple_of(i * ROWS + r, 8), CELL), :] = zeros
        for r in (0, 8, 16, 24):
            cand_s[pl.ds(pl.multiple_of(i * ROWS + r, 8), CELL), :] = zeros
        for r in (8, 24):
            force_rows[pl.ds(pl.multiple_of(i * ROWS + r, 8), CELL), :] = zeros

    load.wait()

    cell = lax.broadcasted_iota(jnp.int32, (slots, bins), 0)
    hot = (cell == dest[...]).astype(BF16)
    hot = jnp.concatenate([hot, hot, hot], axis=1)

    def pack(lo, hi):
        for at in range(lo, hi):
            field = pbuf[pl.ds(ORDER[at], bins, stride=FIELDS), :]
            parts = jnp.concatenate([p.astype(BF16) for p in halves(field, 3)], axis=0)
            outbox[at] = jnp.dot(hot, parts, preferred_element_type=F32)

    mine = pl.ds(pl.multiple_of(tile * CELL, CELL), CELL)
    own_mine = pl.ds(pl.multiple_of(slots + tile * CELL, CELL), CELL)

    def landing(group, rows, own_rows):
        if group == 0:
            return pool1.at[:, own_rows, :]
        if group == 1:
            return pool2.at[:, own_rows, :]
        return carried.at[:, rows, :]

    def send(group):
        lo, hi = GROUPS[group]
        copies = []
        for i in sorted(range(1, n_tile), key=lambda j: -min(j, n_tile - j)):
            peer = lax.rem(tile + i, n_tile)
            theirs = pl.ds(pl.multiple_of(peer * CELL, CELL), CELL)
            copy = pltpu.make_async_remote_copy(
                src_ref=outbox.at[lo:hi, theirs, :],
                dst_ref=landing(group, mine, own_mine),
                send_sem=a2a_send.at[group, i],
                recv_sem=a2a_recv.at[group, i],
                device_id=(slab, peer),
                device_id_type=MESH,
            )
            copy.start()
            copies.append((i, copy))
        here = outbox[lo:hi, mine, :]
        if group == 0:
            pool1[:, own_mine, :] = here
        elif group == 1:
            pool2[:, own_mine, :] = here
        else:
            carried[:, mine, :] = here
        return copies

    def forward(kind, i):
        pool, fields = ((pool1, 5), (pool2, 3))[kind]
        source = lax.rem(tile + n_tile - i, n_tile) if i else tile
        copies = []
        for side, (target, base) in enumerate(((up, 0), (down, 2 * slots))):
            copy = pltpu.make_async_remote_copy(
                src_ref=pool.at[0:fields, pl.ds(pl.multiple_of(slots + source * CELL, CELL), CELL), :],
                dst_ref=pool.at[0:fields, pl.ds(pl.multiple_of(base + source * CELL, CELL), CELL), :],
                send_sem=halo_send.at[kind, side, i],
                recv_sem=halo_recv.at[kind, side, i],
                device_id=(target, tile),
                device_id_type=MESH,
            )
            copy.start()
            copies.append(copy)
        return copies

    def prepare(g, own):
        at = pl.ds(pl.multiple_of(g * CELL, CELL), CELL)
        mass = pool1[3, at, :]
        width = jnp.where(mass > 0, pool1[4, at, :], 1.0)
        masses[at, :] = mass
        s1, s2 = halves(width, 2)
        norm = jnp.zeros((CELL, LANES), F32)

        def put(ref, row, value, group):
            ref[pl.ds(group * CELL * ROWS + row, CELL, stride=ROWS), :] = value

        go = g - groups
        for d in range(3):
            x1, x2 = halves(pool1[d, at, :] - 1.0, 2)
            x = x1 + x2
            xs[d, at, :] = x
            norm = norm + x * x
            for r, (a, c) in enumerate(((x1, x1), (x1, x2), (x2, x1), (x2, x2))):
                put(cand_d, 4 * d + r, -2.0 * c, g)
                if own:
                    put(self_rows, 4 * d + r, a, go)
        for r, n in enumerate(halves(norm, 3)):
            put(cand_d, 12 + r, ones, g)
            put(cand_d, 15 + r, n, g)
            if own:
                put(self_rows, 12 + r, n, go)
                put(self_rows, 15 + r, ones, go)
        put(cand_s, 15, s1, g)
        put(cand_s, 16, s2, g)
        put(cand_s, 18, ones, g)
        put(cand_s, 19, ones, g)
        if own:
            put(self_rows, 18, s1, go)
            put(self_rows, 19, s2, go)

    def tile_rows(ref, j):
        return ref[pl.ds(j * ROWS, ROWS), :].astype(BF16)

    def pair(near, j, place, weight):
        far = jnp.concatenate([tile_rows(cand_d, j), tile_rows(cand_s, j)], axis=1)
        both = jnp.dot(near, far, preferred_element_type=F32)
        square = jnp.maximum(both[:, :LANES], 1e-12)
        s = both[:, LANES:]
        z = lax.rsqrt(square * (s * s))
        u = square * z
        i2 = z * u
        e = jnp.maximum(1.0 - u, 0.0)
        e2 = e * e
        g = (e2 * e) * (i2 * i2 * s)
        w = g * (e - 0.8 * e2)
        slope = g * i2
        high = slope.astype(BF16)
        low = (slope - high.astype(F32)).astype(BF16)
        slopes[place, :, 0:LANES] = high
        slopes[place, :, LANES:] = low
        mass = masses[j][None, :] * weight
        return w * mass

    def total(w):
        high = w.astype(BF16)
        low = (w - high.astype(F32)).astype(BF16)
        stacked = jnp.concatenate([high, low], axis=1)
        row = lax.dot_general(
            jnp.full((16, 2 * LANES), 1.0, BF16), stacked, (((1,), (1,)), ((), ())), preferred_element_type=F32
        )
        return row[0:1] * W_SCALE

    def near_of(i):
        return self_rows[pl.ds(i * ROWS, ROWS), :].T.astype(BF16)

    def used(i, k):
        return lax.min(lax.max(cnt[i] - k, 0), 1).astype(F32)

    pack(*GROUPS[0])
    pl.semaphore_wait(barrier, n_tile + 1)
    waiting = send(0)
    forwarded = [forward(0, 0)]
    pack(*GROUPS[1])
    pack(*GROUPS[2])
    arrival = sorted(range(1, n_tile), key=lambda j: min(j, n_tile - j))
    by_offset = dict(waiting)
    for i in arrival:
        by_offset[i].wait_recv()
        forwarded.append(forward(0, i))
    second = send(1)

    @pl.loop(0, groups)
    def _(g):
        prepare(g + groups, True)

    @pl.loop(0, slots)
    def _(i):
        rho[pl.ds(i, 1), :] = total(pair(near_of(i), slots + i, 4 * i, 1.0))

    for copies in forwarded:
        for copy in copies:
            copy.wait_recv()

    @pl.loop(0, groups)
    def _(g):
        prepare(g, False)
        prepare(g + 2 * groups, False)

    third = send(2)
    for _, copy in second:
        copy.wait_recv()
    passed = [forward(1, i) for i in range(n_tile)]

    chunk = min(16, slots)
    r_copies = []

    def density_of(i):
        near = near_of(i)
        w = None
        for k in range(1, 4):
            j = nbr[i, k]
            weight = used(i, k)
            term = pair(near, j, 4 * i + k, weight)
            w = term if w is None else w + term
        rho[pl.ds(i, 1), :] += total(w)

    for c in range(slots // chunk):
        @pl.loop(c * chunk, (c + 1) * chunk)
        def _(i):
            density_of(i)

        for g in range(c * chunk // CELL, (c + 1) * chunk // CELL):
            at = pl.ds(slots + g * CELL, CELL)
            density = rho[pl.ds(g * CELL, CELL), :]
            pressure = (ADIABATIC - 1.0) * density * pool2[3, at, :]
            safe = jnp.where(pool1[3, at, :] > 0, density, 1.0)
            poolr[at, :] = pressure / (safe * safe)
        for side, (target, base) in enumerate(((up, 0), (down, 2 * slots))):
            copy = pltpu.make_async_remote_copy(
                src_ref=poolr.at[slots + c * chunk : slots + (c + 1) * chunk, :],
                dst_ref=poolr.at[base + c * chunk : base + (c + 1) * chunk, :],
                send_sem=r_send.at[side, c],
                recv_sem=r_recv.at[side, c],
                device_id=(target, tile),
                device_id_type=MESH,
            )
            copy.start()
            r_copies.append(copy)

    for copies in passed:
        for copy in copies:
            copy.wait_recv()

    def prepare_force(g):
        at = pl.ds(pl.multiple_of(g * CELL, CELL), CELL)
        mass = pool1[3, at, :]
        x = [xs[d, at, :] for d in range(3)]
        v = [pool2[d, at, :] for d in range(3)]
        massed = mass * poolr[at, :]
        columns = [mass] + [mass * c for c in x] + [massed] + [massed * c for c in x] + [mass * c for c in v]
        columns.append(mass * (x[0] * v[0] + x[1] * v[1] + x[2] * v[2]))
        for r, column in enumerate(columns):
            high, low = halves(column, 2)
            force_rows[pl.ds(g * CELL * ROWS + r, CELL, stride=ROWS), :] = high
            force_rows[pl.ds(g * CELL * ROWS + 16 + r, CELL, stride=ROWS), :] = low

    def pull(j, place, weight):
        rows = (force_rows[pl.ds(j * ROWS, ROWS), :] * weight).astype(BF16)
        out = lax.dot_general(
            jnp.concatenate([rows, rows], axis=1),
            slopes[place],
            (((1,), (1,)), ((), ())),
            preferred_element_type=F32,
        )
        return out[0:16] + out[16:32]

    @pl.loop(0, groups)
    def _(g):
        prepare_force(g + groups)

    @pl.loop(0, slots)
    def _(i):
        sums[pl.ds(pl.multiple_of(i * 16, 16), 16), :] = pull(slots + i, 4 * i, 1.0)

    for copy in r_copies:
        copy.wait_recv()

    @pl.loop(0, groups)
    def _(g):
        prepare_force(g)
        prepare_force(g + 2 * groups)

    @pl.loop(0, slots)
    def _(i):
        t = None
        for k in range(1, 4):
            part = pull(nbr[i, k], 4 * i + k, used(i, k))
            t = part if t is None else t + part
        sums[pl.ds(pl.multiple_of(i * 16, 16), 16), :] += t

    for _, copy in third:
        copy.wait_recv()

    @pl.loop(0, groups)
    def _(g):
        at = pl.ds(pl.multiple_of(g * CELL, CELL), CELL)
        own = pl.ds(pl.multiple_of(slots + g * CELL, CELL), CELL)
        t = [sums[pl.ds(g * CELL * 16 + r, CELL, stride=16), :] * G_SCALE for r in range(12)]
        x = [xs[d, own, :] for d in range(3)]
        v = [pool2[d, own, :] for d in range(3)]
        mass = pool1[3, own, :]
        ratio = poolr[own, :]
        present = jnp.where(mass > 0, 1.0, 0.0)
        accel = [-(ratio * (x[d] * t[0] - t[1 + d]) + (x[d] * t[4] - t[5 + d])) for d in range(3)]
        heat = t[11]
        for d in range(3):
            heat = heat + x[d] * (v[d] * t[0] - t[8 + d]) - v[d] * t[1 + d]
        heat = ratio * heat
        speed = [v[d] + TIMESTEP * accel[d] for d in range(3)]
        place = [pool1[d, own, :] + TIMESTEP * speed[d] for d in range(3)]
        energy = pool2[3, own, :] + TIMESTEP * heat
        fields = place + speed + [mass, energy, pool1[4, own, :]] + [carried[f, at, :] for f in range(7)]
        for f, value in enumerate(fields):
            updated[pl.ds(g * CELL * FIELDS + f, CELL, stride=FIELDS), :] = value * present
        for f, value in enumerate([rho[at, :]] + accel + [heat]):
            value = value * present
            for r in range(CELL):
                derived[g * CELL + r, f : f + 1, :] = value[r : r + 1]

    for copies in (waiting, second, third):
        for _, copy in copies:
            copy.wait_send()
    for copies in forwarded + passed:
        for copy in copies:
            copy.wait_send()
    for copy in r_copies:
        copy.wait_send()


def step(n_slab, n_tile, particles, dest_slot, neighbours, counts):
    slots = n_tile * CELL
    bins = particles.shape[0]
    chunks = slots // min(16, slots)
    dma = pltpu.SemaphoreType.DMA
    vmem = pl.BlockSpec(memory_space=pltpu.VMEM)
    smem = pl.BlockSpec(memory_space=pltpu.SMEM)
    updated, derived = pl.pallas_call(
        functools.partial(kernel, n_slab, n_tile),
        out_shape=(
            jax.ShapeDtypeStruct((slots * FIELDS, LANES), F32),
            jax.ShapeDtypeStruct((slots, 5, LANES), F32),
        ),
        in_specs=[smem, smem, vmem, pl.BlockSpec(memory_space=pl.ANY)],
        out_specs=(vmem, vmem),
        scratch_shapes=[
            pltpu.VMEM((bins * FIELDS, LANES), F32),
            pltpu.VMEM((FIELDS, slots, LANES), F32),
            pltpu.VMEM((5, 3 * slots, LANES), F32),
            pltpu.VMEM((4, 3 * slots, LANES), F32),
            pltpu.VMEM((7, slots, LANES), F32),
            pltpu.VMEM((3 * slots, LANES), F32),
            pltpu.VMEM((3, 3 * slots, LANES), F32),
            pltpu.VMEM((slots * ROWS, LANES), F32),
            pltpu.VMEM((3 * slots * ROWS, LANES), F32),
            pltpu.VMEM((3 * slots * ROWS, LANES), F32),
            pltpu.VMEM((3 * slots * ROWS, LANES), F32),
            pltpu.VMEM((slots * 4, LANES, 2 * LANES), BF16),
            pltpu.VMEM((slots, LANES), F32),
            pltpu.VMEM((slots * 16, LANES), F32),
            pltpu.VMEM((3 * slots, LANES), F32),
            dma,
            dma((3, n_tile)),
            dma((3, n_tile)),
            dma((2, 2, n_tile)),
            dma((2, 2, n_tile)),
            dma((2, chunks)),
            dma((2, chunks)),
        ],
        compiler_params=pltpu.CompilerParams(collective_id=0, has_side_effects=True),
    )(neighbours, counts, dest_slot.reshape(1, bins), particles.reshape(bins * FIELDS, LANES))
    return updated.reshape(slots, FIELDS, LANES), derived


def solution(mesh):
    in_specs = (
        P(("slab", "tile"), None, None),
        P(("slab", "tile")),
        P(("slab", "tile"), None),
        P(("slab", "tile")),
    )
    out_specs = (P(("slab", "tile"), None, None), P(("slab", "tile"), None, None))
    body = functools.partial(step, mesh.shape["slab"], mesh.shape["tile"])
    return jax.shard_map(body, mesh=mesh, in_specs=in_specs, out_specs=out_specs, check_vma=False)
```

```python
import functools
import math

import jax
import jax.numpy as jnp
from jax import lax
from jax.experimental import pallas as pl
from jax.experimental.pallas import tpu as pltpu
from jax.sharding import PartitionSpec as P

ADIABATIC = 5.0 / 3.0
TIMESTEP = 0.5
KERNEL_NORM = 21.0 / (16.0 * math.pi)
W_SCALE = KERNEL_NORM / 2048.0
G_SCALE = -160.0 * KERNEL_NORM / 65536.0

FIELDS = 16
CELL = 8
LANES = 128
ROWS = 32
ORDER = (0, 1, 2, 6, 8, 3, 4, 5, 7, 9, 10, 11, 12, 13, 14, 15)
GROUPS = ((0, 5), (5, 9), (9, 16))
F32 = jnp.float32
BF16 = jnp.bfloat16
MESH = pl.DeviceIdType.MESH


def halves(x, count):
    parts = []
    for _ in range(count - 1):
        part = x.astype(BF16).astype(F32)
        parts.append(part)
        x = x - part
    parts.append(x.astype(BF16).astype(F32))
    return parts


def kernel(
    n_slab,
    n_tile,
    nbr,
    cnt,
    dest,
    particles,
    updated,
    derived,
    pbuf,
    outbox,
    pool1,
    pool2,
    carried,
    poolr,
    xs,
    self_rows,
    cand_d,
    cand_s,
    force_rows,
    slopes,
    rho,
    sums,
    masses,
    turned,
    even,
    odd,
    columns,
    in_sem,
    a2a_send,
    a2a_recv,
    halo_send,
    halo_recv,
    r_send,
    r_recv,
):
    slots = n_tile * CELL
    bins = pbuf.shape[0] // FIELDS
    groups = slots // CELL
    slab = lax.axis_index("slab")
    tile = lax.axis_index("tile")
    up = lax.rem(slab + 1, n_slab)
    down = lax.rem(slab + n_slab - 1, n_slab)

    load = pltpu.make_async_copy(particles, pbuf, in_sem)
    load.start()

    barrier = pltpu.get_barrier_semaphore()
    for i in range(1, n_tile):
        peer = lax.rem(tile + i, n_tile)
        pl.semaphore_signal(barrier, inc=1, device_id=(slab, peer), device_id_type=MESH)
    for side in (up, down):
        pl.semaphore_signal(barrier, inc=1, device_id=(side, tile), device_id_type=MESH)

    zeros = jnp.zeros((CELL, LANES), F32)
    ones = jnp.ones((CELL, LANES), F32)

    @pl.loop(0, slots)
    def _(i):
        for r in (16, 24):
            self_rows[pl.ds(pl.multiple_of(i * ROWS + r, 8), CELL), :] = zeros

    @pl.loop(0, 3 * slots)
    def _(i):
        for r in (16, 24):
            cand_d[pl.ds(pl.multiple_of(i * ROWS + r, 8), CELL), :] = zeros
        for r in (0, 8, 16, 24):
            cand_s[pl.ds(pl.multiple_of(i * ROWS + r, 8), CELL), :] = zeros
        for r in (8, 24):
            force_rows[pl.ds(pl.multiple_of(i * ROWS + r, 8), CELL), :] = zeros

    load.wait()

    cell = lax.broadcasted_iota(jnp.int32, (slots, bins), 0)
    hot = (cell == dest[...]).astype(BF16)
    hot = jnp.concatenate([hot, hot, hot], axis=1)

    def pack(lo, hi):
        for at in range(lo, hi):
            field = pbuf[pl.ds(ORDER[at], bins, stride=FIELDS), :]
            parts = jnp.concatenate([p.astype(BF16) for p in halves(field, 3)], axis=0)
            outbox[at] = jnp.dot(hot, parts, preferred_element_type=F32)

    mine = pl.ds(pl.multiple_of(tile * CELL, CELL), CELL)
    own_mine = pl.ds(pl.multiple_of(slots + tile * CELL, CELL), CELL)

    def landing(group, rows, own_rows):
        if group == 0:
            return pool1.at[:, own_rows, :]
        if group == 1:
            return pool2.at[:, own_rows, :]
        return carried.at[:, rows, :]

    def send(group):
        lo, hi = GROUPS[group]
        copies = []
        for i in sorted(range(1, n_tile), key=lambda j: -min(j, n_tile - j)):
            peer = lax.rem(tile + i, n_tile)
            theirs = pl.ds(pl.multiple_of(peer * CELL, CELL), CELL)
            copy = pltpu.make_async_remote_copy(
                src_ref=outbox.at[lo:hi, theirs, :],
                dst_ref=landing(group, mine, own_mine),
                send_sem=a2a_send.at[group, i],
                recv_sem=a2a_recv.at[group, i],
                device_id=(slab, peer),
                device_id_type=MESH,
            )
            copy.start()
            copies.append((i, copy))
        here = outbox[lo:hi, mine, :]
        if group == 0:
            pool1[:, own_mine, :] = here
        elif group == 1:
            pool2[:, own_mine, :] = here
        else:
            carried[:, mine, :] = here
        return copies

    def forward(kind, i):
        pool, fields = ((pool1, 5), (pool2, 3))[kind]
        source = lax.rem(tile + n_tile - i, n_tile) if i else tile
        copies = []
        for side, (target, base) in enumerate(((up, 0), (down, 2 * slots))):
            copy = pltpu.make_async_remote_copy(
                src_ref=pool.at[0:fields, pl.ds(pl.multiple_of(slots + source * CELL, CELL), CELL), :],
                dst_ref=pool.at[0:fields, pl.ds(pl.multiple_of(base + source * CELL, CELL), CELL), :],
                send_sem=halo_send.at[kind, side, i],
                recv_sem=halo_recv.at[kind, side, i],
                device_id=(target, tile),
                device_id_type=MESH,
            )
            copy.start()
            copies.append(copy)
        return copies

    def prepare(g, own):
        at = pl.ds(pl.multiple_of(g * CELL, CELL), CELL)
        mass = pool1[3, at, :]
        width = jnp.where(mass > 0, pool1[4, at, :], 1.0)
        masses[at, :] = mass
        q1, q2 = halves(0.25 * width, 2)
        q = q1 + q2
        norm = jnp.zeros((CELL, LANES), F32)

        def put(ref, row, value, group):
            ref[pl.ds(group * CELL * ROWS + row, CELL, stride=ROWS), :] = value

        go = g - groups
        for d in range(3):
            x1, x2 = halves(pool1[d, at, :] - 1.0, 2)
            x = x1 + x2
            xs[d, at, :] = x
            norm = norm + x * x
            for r, (a, c) in enumerate(((x1, x1), (x1, x2), (x2, x1), (x2, x2))):
                put(cand_d, 4 * d + r, -2.0 * c, g)
                if own:
                    put(self_rows, 4 * d + r, a, go)
        for r, n in enumerate(halves(norm, 3)):
            put(cand_d, 12 + r, ones, g)
            put(cand_d, 15 + r, n, g)
            if own:
                put(self_rows, 12 + r, n, go)
                put(self_rows, 15 + r, ones, go)
        for r, n in enumerate(halves(q * q, 3)):
            put(cand_s, 15 + r, n, g)
            put(cand_s, 18 + r, ones, g)
            if own:
                put(self_rows, 18 + r, n, go)
        for r, (a, c) in enumerate(((q1, q1), (q1, q2), (q2, q1), (q2, q2))):
            put(cand_s, 21 + r, 2.0 * c, g)
            if own:
                put(self_rows, 21 + r, a, go)

    def tile_rows(ref, j):
        return ref[pl.ds(j * ROWS, ROWS), :].astype(BF16)

    lane = lax.broadcasted_iota(jnp.int32, (ROWS, LANES), 1)

    def measure(buffer, t, block, r, j):
        far = jnp.concatenate([tile_rows(cand_d, j), tile_rows(cand_s, j)], axis=1)
        parts = [far]
        if r > 0:
            parts.insert(0, jnp.zeros((r * ROWS, 2 * LANES), BF16))
        if r < 3:
            parts.append(jnp.zeros(((3 - r) * ROWS, 2 * LANES), BF16))
        buffer[t] = jnp.dot(turned[block], jnp.concatenate(parts, axis=0), preferred_element_type=F32)

    def weigh(buffer, i, tiles):
        for at in range(0, LANES, ROWS):
            rows = slice(at, at + ROWS)
            w = None
            for t, place, mass in tiles:
                square = jnp.maximum(buffer[t, rows, 0:LANES], 1e-12)
                inv = lax.rsqrt(buffer[t, rows, LANES:])
                e = jnp.maximum(4.0 - (square * lax.rsqrt(square)) * inv, 0.0)
                h = e * inv
                g = (h * h) * h
                slope = g * (inv * inv)
                high = slope.astype(BF16)
                slopes[place, rows, 0:LANES] = high
                slopes[place, rows, LANES:] = (slope - high.astype(F32)).astype(BF16)
                term = (g * (e * (5.0 - e))) * mass
                w = term if w is None else w + term
            column = jnp.sum(w, axis=1, keepdims=True)
            columns[rows, :] += jnp.where(lane == i, column, 0.0)

    def used(i, k):
        return lax.min(lax.max(cnt[i] - k, 0), 1).astype(F32)

    pack(*GROUPS[0])
    pl.semaphore_wait(barrier, n_tile + 1)
    waiting = send(0)
    forwarded = [forward(0, 0)]
    pack(*GROUPS[1])
    pack(*GROUPS[2])
    arrival = sorted(range(1, n_tile), key=lambda j: min(j, n_tile - j))
    by_offset = dict(waiting)
    for i in arrival:
        by_offset[i].wait_recv()
        forwarded.append(forward(0, i))
    second = send(1)

    @pl.loop(0, groups)
    def _(g):
        prepare(g + groups, True)

    columns[...] = jnp.zeros((LANES, LANES), F32)

    @pl.loop(0, slots // 4)
    def _(b):
        turned[b] = self_rows[pl.ds(pl.multiple_of(b * LANES, LANES), LANES), :].T.astype(BF16)

    def self_measure(buffer, b):
        for r in range(4):
            measure(buffer, r, b, r, slots + 4 * b + r)

    def self_weigh(buffer, b):
        for r in range(4):
            i = 4 * b + r
            weigh(buffer, i, [(r, 4 * i, masses[slots + i][None, :])])

    self_measure(even, 0)

    @pl.loop(0, slots // 8)
    def _(p):
        self_measure(odd, 2 * p + 1)
        self_weigh(even, 2 * p)
        self_measure(even, lax.min(2 * p + 2, slots // 4 - 1))
        self_weigh(odd, 2 * p + 1)

    for copies in forwarded:
        for copy in copies:
            copy.wait_recv()

    @pl.loop(0, groups)
    def _(g):
        prepare(g, False)
        prepare(g + 2 * groups, False)

    third = send(2)
    for _, copy in second:
        copy.wait_recv()
    passed = [forward(1, i) for i in range(n_tile)]

    chunk = slots // 2

    def others_measure(buffer, b, r):
        for k in range(1, 4):
            measure(buffer, k - 1, b, r, nbr[k, 4 * b + r])

    def others_weigh(buffer, b, r):
        i = 4 * b + r
        tiles = []
        for k in range(1, 4):
            tiles.append((k - 1, 4 * i + k, masses[nbr[k, i]][None, :] * used(i, k)))
        weigh(buffer, i, tiles)

    def ratio_copies(c):
        rows = pl.multiple_of(c * chunk, CELL)
        return [
            pltpu.make_async_remote_copy(
                src_ref=poolr.at[pl.ds(slots + rows, chunk), :],
                dst_ref=poolr.at[pl.ds(base + rows, chunk), :],
                send_sem=r_send.at[side, c],
                recv_sem=r_recv.at[side, c],
                device_id=(target, tile),
                device_id_type=MESH,
            )
            for side, (target, base) in enumerate(((up, 0), (down, 2 * slots)))
        ]

    others_measure(even, 0, 0)

    @pl.loop(0, 2)
    def _(c):
        @pl.loop(0, chunk // 4)
        def _(p):
            b = c * (chunk // 4) + p
            for r in range(4):
                ahead, now = (odd, even) if r % 2 == 0 else (even, odd)
                if r < 3:
                    others_measure(ahead, b, r + 1)
                else:
                    others_measure(ahead, lax.min(b + 1, slots // 4 - 1), 0)
                others_weigh(now, b, r)

        rho[...] = columns[...].T * W_SCALE

        @pl.loop(0, chunk // CELL)
        def _(p):
            row = pl.multiple_of(c * chunk + p * CELL, CELL)
            at = pl.ds(slots + row, CELL)
            density = rho[pl.ds(row, CELL), :]
            pressure = (ADIABATIC - 1.0) * density * pool2[3, at, :]
            safe = jnp.where(pool1[3, at, :] > 0, density, 1.0)
            poolr[at, :] = pressure / (safe * safe)

        for copy in ratio_copies(c):
            copy.start()

    r_copies = ratio_copies(0) + ratio_copies(1)

    for copies in passed:
        for copy in copies:
            copy.wait_recv()

    def prepare_force(g):
        at = pl.ds(pl.multiple_of(g * CELL, CELL), CELL)
        mass = pool1[3, at, :]
        x = [xs[d, at, :] for d in range(3)]
        v = [pool2[d, at, :] for d in range(3)]
        massed = mass * poolr[at, :]
        columns = [mass] + [mass * c for c in x] + [massed] + [massed * c for c in x] + [mass * c for c in v]
        columns.append(mass * (x[0] * v[0] + x[1] * v[1] + x[2] * v[2]))
        for r, column in enumerate(columns):
            high, low = halves(column, 2)
            force_rows[pl.ds(g * CELL * ROWS + r, CELL, stride=ROWS), :] = high
            force_rows[pl.ds(g * CELL * ROWS + 16 + r, CELL, stride=ROWS), :] = low

    def pull(tiles):
        lefts, rights = [], []
        for j, place, weight in tiles:
            rows = (force_rows[pl.ds(j * ROWS, ROWS), :] * weight).astype(BF16)
            lefts += [rows, rows]
            rights.append(slopes[place])
        out = lax.dot_general(
            jnp.concatenate(lefts, axis=1),
            jnp.concatenate(rights, axis=1),
            (((1,), (1,)), ((), ())),
            preferred_element_type=F32,
        )
        return out[0:16] + out[16:32]

    @pl.loop(0, groups)
    def _(g):
        prepare_force(g + groups)

    @pl.loop(0, slots // 8)
    def _(b):
        for r in range(8):
            i = 8 * b + r
            sums[pl.ds(pl.multiple_of(i * 16, 16), 16), :] = pull([(slots + i, 4 * i, 1.0)])

    for copy in r_copies:
        copy.wait_recv()

    @pl.loop(0, groups)
    def _(g):
        prepare_force(g)
        prepare_force(g + 2 * groups)

    @pl.loop(0, slots // 4)
    def _(b):
        for r in range(4):
            i = 4 * b + r
            tiles = [(nbr[k, i], 4 * i + k, used(i, k)) for k in range(1, 4)]
            sums[pl.ds(pl.multiple_of(i * 16, 16), 16), :] += pull(tiles)

    for _, copy in third:
        copy.wait_recv()

    @pl.loop(0, groups)
    def _(g):
        at = pl.ds(pl.multiple_of(g * CELL, CELL), CELL)
        own = pl.ds(pl.multiple_of(slots + g * CELL, CELL), CELL)
        t = [sums[pl.ds(g * CELL * 16 + r, CELL, stride=16), :] * G_SCALE for r in range(12)]
        x = [xs[d, own, :] for d in range(3)]
        v = [pool2[d, own, :] for d in range(3)]
        mass = pool1[3, own, :]
        ratio = poolr[own, :]
        present = jnp.where(mass > 0, 1.0, 0.0)
        accel = [-(ratio * (x[d] * t[0] - t[1 + d]) + (x[d] * t[4] - t[5 + d])) for d in range(3)]
        heat = t[11]
        for d in range(3):
            heat = heat + x[d] * (v[d] * t[0] - t[8 + d]) - v[d] * t[1 + d]
        heat = ratio * heat
        speed = [v[d] + TIMESTEP * accel[d] for d in range(3)]
        place = [pool1[d, own, :] + TIMESTEP * speed[d] for d in range(3)]
        energy = pool2[3, own, :] + TIMESTEP * heat
        fields = place + speed + [mass, energy, pool1[4, own, :]] + [carried[f, at, :] for f in range(7)]
        for f, value in enumerate(fields):
            updated[pl.ds(g * CELL * FIELDS + f, CELL, stride=FIELDS), :] = value * present
        for f, value in enumerate([rho[at, :]] + accel + [heat]):
            derived[f, at, :] = value * present

    for copies in (waiting, second, third):
        for _, copy in copies:
            copy.wait_send()
    for copies in forwarded + passed:
        for copy in copies:
            copy.wait_send()
    for copy in r_copies:
        copy.wait_send()


def step(n_slab, n_tile, particles, dest_slot, neighbours, counts):
    slots = n_tile * CELL
    bins = particles.shape[0]
    dma = pltpu.SemaphoreType.DMA
    vmem = pl.BlockSpec(memory_space=pltpu.VMEM)
    smem = pl.BlockSpec(memory_space=pltpu.SMEM)
    updated, derived = pl.pallas_call(
        functools.partial(kernel, n_slab, n_tile),
        out_shape=(
            jax.ShapeDtypeStruct((slots * FIELDS, LANES), F32),
            jax.ShapeDtypeStruct((5, slots, LANES), F32),
        ),
        in_specs=[smem, smem, vmem, pl.BlockSpec(memory_space=pl.ANY)],
        out_specs=(vmem, vmem),
        scratch_shapes=[
            pltpu.VMEM((bins * FIELDS, LANES), F32),
            pltpu.VMEM((FIELDS, slots, LANES), F32),
            pltpu.VMEM((5, 3 * slots, LANES), F32),
            pltpu.VMEM((4, 3 * slots, LANES), F32),
            pltpu.VMEM((7, slots, LANES), F32),
            pltpu.VMEM((3 * slots, LANES), F32),
            pltpu.VMEM((3, 3 * slots, LANES), F32),
            pltpu.VMEM((slots * ROWS, LANES), F32),
            pltpu.VMEM((3 * slots * ROWS, LANES), F32),
            pltpu.VMEM((3 * slots * ROWS, LANES), F32),
            pltpu.VMEM((3 * slots * ROWS, LANES), F32),
            pltpu.VMEM((slots * 4, LANES, 2 * LANES), BF16),
            pltpu.VMEM((LANES, LANES), F32),
            pltpu.VMEM((slots * 16, LANES), F32),
            pltpu.VMEM((3 * slots, LANES), F32),
            pltpu.VMEM((slots // 4, LANES, LANES), BF16),
            pltpu.VMEM((4, LANES, 2 * LANES), F32),
            pltpu.VMEM((4, LANES, 2 * LANES), F32),
            pltpu.VMEM((LANES, LANES), F32),
            dma,
            dma((3, n_tile)),
            dma((3, n_tile)),
            dma((2, 2, n_tile)),
            dma((2, 2, n_tile)),
            dma((2, 2)),
            dma((2, 2)),
        ],
        compiler_params=pltpu.CompilerParams(collective_id=0, has_side_effects=True),
    )(neighbours.T, counts, dest_slot.reshape(1, bins), particles.reshape(bins * FIELDS, LANES))
    return updated.reshape(slots, FIELDS, LANES), derived.transpose(1, 0, 2)


def solution(mesh):
    in_specs = (
        P(("slab", "tile"), None, None),
        P(("slab", "tile")),
        P(("slab", "tile"), None),
        P(("slab", "tile")),
    )
    out_specs = (P(("slab", "tile"), None, None), P(("slab", "tile"), None, None))
    body = functools.partial(step, mesh.shape["slab"], mesh.shape["tile"])
    return jax.shard_map(body, mesh=mesh, in_specs=in_specs, out_specs=out_specs, check_vma=False)
```

```python
import functools
import math

import jax
import jax.numpy as jnp
from jax import lax
from jax.experimental import pallas as pl
from jax.experimental.pallas import tpu as pltpu
from jax.sharding import PartitionSpec as P

ADIABATIC = 5.0 / 3.0
TIMESTEP = 0.5
KERNEL_NORM = 21.0 / (16.0 * math.pi)
W_SCALE = KERNEL_NORM / 2048.0
G_SCALE = -160.0 * KERNEL_NORM / 65536.0

FIELDS = 16
CELL = 8
LANES = 128
ROWS = 32
ORDER = (0, 1, 2, 6, 8, 3, 4, 5, 7, 9, 10, 11, 12, 13, 14, 15)
GROUPS = ((0, 5), (5, 9), (9, 16))
F32 = jnp.float32
BF16 = jnp.bfloat16
MESH = pl.DeviceIdType.MESH


def halves(x, count):
    parts = []
    for _ in range(count - 1):
        part = x.astype(BF16).astype(F32)
        parts.append(part)
        x = x - part
    parts.append(x.astype(BF16).astype(F32))
    return parts


def kernel(
    n_slab,
    n_tile,
    nbr_in,
    cnt_in,
    dest_in,
    particles,
    updated,
    derived,
    nbr,
    cnt,
    dest,
    pbuf,
    outbox,
    pool1,
    pool2,
    carried,
    poolr,
    xs,
    self_rows,
    cand_d,
    cand_s,
    force_rows,
    slopes,
    rho,
    sums,
    masses,
    turned,
    even,
    odd,
    columns,
    in_sem,
    a2a_send,
    a2a_recv,
    halo_send,
    halo_recv,
    r_send,
    r_recv,
):
    slots = n_tile * CELL
    bins = pbuf.shape[0] // FIELDS
    groups = slots // CELL
    slab = lax.axis_index("slab")
    tile = lax.axis_index("tile")
    up = lax.rem(slab + 1, n_slab)
    down = lax.rem(slab + n_slab - 1, n_slab)

    barrier = pltpu.get_barrier_semaphore()
    for i in range(1, n_tile):
        peer = lax.rem(tile + i, n_tile)
        pl.semaphore_signal(barrier, inc=1, device_id=(slab, peer), device_id_type=MESH)
    for side in (up, down):
        pl.semaphore_signal(barrier, inc=1, device_id=(side, tile), device_id_type=MESH)

    loads = []
    for n, (source, target) in enumerate(((particles, pbuf), (dest_in, dest), (nbr_in, nbr), (cnt_in, cnt))):
        loads.append(pltpu.make_async_copy(source, target, in_sem.at[n]))
        loads[-1].start()

    zeros = jnp.zeros((CELL, LANES), F32)
    ones = jnp.ones((CELL, LANES), F32)
    depth = lax.broadcasted_iota(jnp.int32, (CELL, LANES), 0)

    def spread(ref, row):
        return (row // CELL) * (ref.shape[0] // 4)

    def constants():
        late = jnp.where(depth >= 4, 1.0, 0.0)
        early = jnp.where(depth < 2, 1.0, 0.0)
        middle = jnp.where((depth >= 2) & (depth < 5), 1.0, 0.0)
        fills = ((self_rows, slots, {1: late, 2: early, 3: zeros}),)
        fills += ((cand_d, 3 * slots, {1: late, 2: zeros, 3: zeros}),)
        fills += ((cand_s, 3 * slots, {0: zeros, 1: zeros, 2: middle, 3: zeros}),)
        fills += ((force_rows, 3 * slots, {1: zeros, 3: zeros}),)
        for ref, count, blocks in fills:

            @pl.loop(0, count // 8)
            def _(i):
                for r in range(8):
                    for kb, value in blocks.items():
                        ref[pl.ds(pl.multiple_of((kb * count + 8 * i + r) * CELL, CELL), CELL), :] = value

    loads[0].wait()
    loads[1].wait()

    cell = lax.broadcasted_iota(jnp.int32, (slots, bins), 0)
    hot = (cell == dest[...]).astype(BF16)
    hot = jnp.concatenate([hot, hot, hot], axis=1)

    def pack(lo, hi):
        for at in range(lo, hi):
            field = pbuf[pl.ds(ORDER[at], bins, stride=FIELDS), :]
            parts = jnp.concatenate([p.astype(BF16) for p in halves(field, 3)], axis=0)
            outbox[at] = jnp.dot(hot, parts, preferred_element_type=F32)

    mine = pl.ds(pl.multiple_of(tile * CELL, CELL), CELL)
    own_mine = pl.ds(pl.multiple_of(slots + tile * CELL, CELL), CELL)

    def landing(group, rows, own_rows):
        if group == 0:
            return pool1.at[:, own_rows, :]
        if group == 1:
            return pool2.at[:, own_rows, :]
        return carried.at[:, rows, :]

    def send(group):
        lo, hi = GROUPS[group]
        copies = []
        for i in sorted(range(1, n_tile), key=lambda j: -min(j, n_tile - j)):
            peer = lax.rem(tile + i, n_tile)
            theirs = pl.ds(pl.multiple_of(peer * CELL, CELL), CELL)
            copy = pltpu.make_async_remote_copy(
                src_ref=outbox.at[lo:hi, theirs, :],
                dst_ref=landing(group, mine, own_mine),
                send_sem=a2a_send.at[group, i],
                recv_sem=a2a_recv.at[group, i],
                device_id=(slab, peer),
                device_id_type=MESH,
            )
            copy.start()
            copies.append((i, copy))
        pltpu.make_async_copy(
            outbox.at[lo:hi, mine, :], landing(group, mine, own_mine), a2a_recv.at[group, 0]
        ).start()
        return copies

    def settle(group):
        lo, hi = GROUPS[group]
        pltpu.make_async_copy(
            outbox.at[lo:hi, mine, :], landing(group, mine, own_mine), a2a_recv.at[group, 0]
        ).wait()

    def forward(kind, i):
        pool, fields = ((pool1, 5), (pool2, 3))[kind]
        source = lax.rem(tile + n_tile - i, n_tile) if i else tile
        copies = []
        for side, (target, base) in enumerate(((up, 0), (down, 2 * slots))):
            copy = pltpu.make_async_remote_copy(
                src_ref=pool.at[0:fields, pl.ds(pl.multiple_of(slots + source * CELL, CELL), CELL), :],
                dst_ref=pool.at[0:fields, pl.ds(pl.multiple_of(base + source * CELL, CELL), CELL), :],
                send_sem=halo_send.at[kind, side, i],
                recv_sem=halo_recv.at[kind, side, i],
                device_id=(target, tile),
                device_id_type=MESH,
            )
            copy.start()
            copies.append(copy)
        return copies

    def prepare(g, own):
        at = pl.ds(pl.multiple_of(g * CELL, CELL), CELL)
        mass = pool1[3, at, :]
        width = jnp.where(mass > 0, pool1[4, at, :], 1.0)
        masses[at, :] = mass
        q1, q2 = halves(0.25 * width, 2)
        q = q1 + q2
        norm = jnp.zeros((CELL, LANES), F32)

        def put(ref, row, value, group):
            ref[pl.ds(spread(ref, row) + group * CELL * CELL + row % CELL, CELL, stride=CELL), :] = value

        go = g - groups
        for d in range(3):
            x1, x2 = halves(pool1[d, at, :] - 1.0, 2)
            x = x1 + x2
            xs[d, at, :] = x
            norm = norm + x * x
            for r, (a, c) in enumerate(((x1, x1), (x1, x2), (x2, x1), (x2, x2))):
                put(cand_d, 4 * d + r, -2.0 * c, g)
                if own:
                    put(self_rows, 4 * d + r, a, go)
        for r, n in enumerate(halves(norm, 3)):
            put(cand_d, 15 + r, n, g)
            if own:
                put(self_rows, 12 + r, n, go)
        for r, n in enumerate(halves(q * q, 3)):
            put(cand_s, 15 + r, n, g)
            if own:
                put(self_rows, 18 + r, n, go)
        for r, (a, c) in enumerate(((q1, q1), (q1, q2), (q2, q1), (q2, q2))):
            put(cand_s, 21 + r, 2.0 * c, g)
            if own:
                put(self_rows, 21 + r, a, go)

    def slot_rows(ref, j):
        count = ref.shape[0] // 4
        return jnp.concatenate([ref[pl.ds(kb * count + j * CELL, CELL), :] for kb in range(4)], axis=0)

    def tile_rows(ref, j):
        return slot_rows(ref, j).astype(BF16)

    lane = lax.broadcasted_iota(jnp.int32, (ROWS, LANES), 1)

    def measure(buffer, t, block, r, j):
        far = jnp.concatenate([tile_rows(cand_d, j), tile_rows(cand_s, j)], axis=1)
        parts = [far]
        if r > 0:
            parts.insert(0, jnp.zeros((r * ROWS, 2 * LANES), BF16))
        if r < 3:
            parts.append(jnp.zeros(((3 - r) * ROWS, 2 * LANES), BF16))
        buffer[t] = jnp.dot(turned[block], jnp.concatenate(parts, axis=0), preferred_element_type=F32)

    def weigh(buffer, i, tiles):
        for at in range(0, LANES, ROWS):
            rows = slice(at, at + ROWS)
            w = None
            for t, place, mass in tiles:
                square = jnp.maximum(buffer[t, rows, 0:LANES], 1e-12)
                inv = lax.rsqrt(buffer[t, rows, LANES:])
                e = jnp.maximum(4.0 - (square * lax.rsqrt(square)) * inv, 0.0)
                h = e * inv
                g = (h * h) * h
                slope = g * (inv * inv)
                slopes[place, rows, :] = slope
                term = (g * (e * (5.0 - e))) * mass
                w = term if w is None else w + term
            column = jnp.sum(w, axis=1, keepdims=True)
            columns[rows, :] += jnp.where(lane == i, column, 0.0)

    def used(i, k):
        return lax.min(lax.max(cnt[i] - k, 0), 1).astype(F32)

    def offset_of(n):
        odd = lax.rem(n, 2)
        return odd * lax.div(n + 1, 2) + (1 - odd) * lax.rem(n_tile - lax.div(n, 2), n_tile)

    def source_of(n):
        return lax.rem(tile + n_tile - offset_of(n), n_tile)

    def self_measure(buffer, b):
        for r in range(4):
            measure(buffer, r, b, r, slots + 4 * b + r)

    def self_weigh(buffer, b):
        for r in range(4):
            i = 4 * b + r
            weigh(buffer, i, [(r, 4 * i, masses[slots + i][None, :])])

    def against_self(lo, hi):
        @pl.loop(lo, hi)
        def _(n):
            source = source_of(n)
            prepare(source + groups, True)

        @pl.loop(lo, hi)
        def _(n):
            for h in range(2):
                b = 2 * source_of(n) + h
                rows = [slot_rows(self_rows, 4 * b + r) for r in range(4)]
                turned[b] = jnp.concatenate(rows, axis=0).T.astype(BF16)

        self_measure(even, 2 * source_of(jnp.int32(lo)))

        @pl.loop(lo, hi)
        def _(n):
            b = 2 * source_of(n)
            self_measure(odd, b + 1)
            self_weigh(even, b)
            self_measure(even, 2 * source_of(lax.min(n + 1, hi - 1)))
            self_weigh(odd, b + 1)

    pack(*GROUPS[0])
    pl.semaphore_wait(barrier, n_tile + 1)
    waiting = send(0)
    by_offset = dict(waiting)
    columns[...] = jnp.zeros((LANES, LANES), F32)
    constants()
    pack(*GROUPS[1])
    pack(*GROUPS[2])
    settle(0)
    forwarded = [forward(0, 0)]
    second = []
    cuts = sorted({min(c, n_tile) for c in (0, 3, 5, 8)} | {n_tile})
    for lo, hi in zip(cuts[:-1], cuts[1:]):
        for n in range(max(lo, 1), hi):
            i = (n + 1) // 2 if n % 2 else n_tile - n // 2
            by_offset[i].wait_recv()
            forwarded.append(forward(0, i))
        if hi == n_tile:
            second = send(1)
        against_self(lo, hi)

    for copies in forwarded:
        for copy in copies:
            copy.wait_recv()

    @pl.loop(0, groups)
    def _(g):
        prepare(g, False)
        prepare(g + 2 * groups, False)

    third = send(2)
    settle(1)
    for _, copy in second:
        copy.wait_recv()
    for load in loads[2:]:
        load.wait()
    passed = [forward(1, i) for i in range(n_tile)]

    chunk = slots // 2

    def others_measure(buffer, b, r):
        for k in range(1, 4):
            measure(buffer, k - 1, b, r, nbr[k, 4 * b + r])

    def others_weigh(buffer, b, r):
        i = 4 * b + r
        tiles = []
        for k in range(1, 4):
            tiles.append((k - 1, 4 * i + k, masses[nbr[k, i]][None, :] * used(i, k)))
        weigh(buffer, i, tiles)

    def ratio_copies(c):
        rows = pl.multiple_of(c * chunk, CELL)
        return [
            pltpu.make_async_remote_copy(
                src_ref=poolr.at[pl.ds(slots + rows, chunk), :],
                dst_ref=poolr.at[pl.ds(base + rows, chunk), :],
                send_sem=r_send.at[side, c],
                recv_sem=r_recv.at[side, c],
                device_id=(target, tile),
                device_id_type=MESH,
            )
            for side, (target, base) in enumerate(((up, 0), (down, 2 * slots)))
        ]

    others_measure(even, 0, 0)

    @pl.loop(0, 2)
    def _(c):
        @pl.loop(0, chunk // 4)
        def _(p):
            b = c * (chunk // 4) + p
            for r in range(4):
                ahead, now = (odd, even) if r % 2 == 0 else (even, odd)
                if r < 3:
                    others_measure(ahead, b, r + 1)
                else:
                    others_measure(ahead, lax.min(b + 1, slots // 4 - 1), 0)
                others_weigh(now, b, r)

        rho[...] = columns[...].T * W_SCALE

        @pl.loop(0, chunk // CELL)
        def _(p):
            row = pl.multiple_of(c * chunk + p * CELL, CELL)
            at = pl.ds(slots + row, CELL)
            density = rho[pl.ds(row, CELL), :]
            pressure = (ADIABATIC - 1.0) * density * pool2[3, at, :]
            safe = jnp.where(pool1[3, at, :] > 0, density, 1.0)
            poolr[at, :] = pressure / (safe * safe)

        for copy in ratio_copies(c):
            copy.start()

    r_copies = ratio_copies(0) + ratio_copies(1)

    for copies in passed:
        for copy in copies:
            copy.wait_recv()

    def put_force(row, g, value):
        high, low = halves(value, 2)
        for base, part in ((row, high), (row + 16, low)):
            at = pl.ds(spread(force_rows, base) + g * CELL * CELL + base % CELL, CELL, stride=CELL)
            force_rows[at, :] = part

    def prepare_motion(g):
        at = pl.ds(pl.multiple_of(g * CELL, CELL), CELL)
        mass = pool1[3, at, :]
        x = [xs[d, at, :] for d in range(3)]
        v = [pool2[d, at, :] for d in range(3)]
        put_force(0, g, mass)
        for d in range(3):
            put_force(1 + d, g, mass * x[d])
            put_force(8 + d, g, mass * v[d])
        put_force(11, g, mass * (x[0] * v[0] + x[1] * v[1] + x[2] * v[2]))

    def prepare_ratio(g):
        at = pl.ds(pl.multiple_of(g * CELL, CELL), CELL)
        massed = pool1[3, at, :] * poolr[at, :]
        put_force(4, g, massed)
        for d in range(3):
            put_force(5 + d, g, massed * xs[d, at, :])

    def pull(tiles):
        lefts, rights = [], []
        for j, place, weight in tiles:
            rows = (slot_rows(force_rows, j) * weight).astype(BF16)
            slope = slopes[place]
            high = slope.astype(BF16)
            lefts += [rows, rows]
            rights += [high, (slope - high.astype(F32)).astype(BF16)]
        out = lax.dot_general(
            jnp.concatenate(lefts, axis=1),
            jnp.concatenate(rights, axis=1),
            (((1,), (1,)), ((), ())),
            preferred_element_type=F32,
        )
        return out[0:16] + out[16:32]

    @pl.loop(0, groups)
    def _(g):
        prepare_motion(g + groups)
        prepare_ratio(g + groups)

    @pl.loop(0, slots // 16)
    def _(b):
        for r in range(16):
            i = 16 * b + r
            sums[pl.ds(pl.multiple_of(i * 16, 16), 16), :] = pull([(slots + i, 4 * i, 1.0)])

    @pl.loop(0, groups)
    def _(g):
        prepare_motion(g)
        prepare_motion(g + 2 * groups)

    for copy in r_copies:
        copy.wait_recv()

    @pl.loop(0, groups)
    def _(g):
        prepare_ratio(g)
        prepare_ratio(g + 2 * groups)

    @pl.loop(0, slots // 8)
    def _(b):
        for r in range(8):
            i = 8 * b + r
            tiles = [(nbr[k, i], 4 * i + k, used(i, k)) for k in range(1, 4)]
            sums[pl.ds(pl.multiple_of(i * 16, 16), 16), :] += pull(tiles)

    settle(2)
    for _, copy in third:
        copy.wait_recv()

    @pl.loop(0, groups)
    def _(g):
        at = pl.ds(pl.multiple_of(g * CELL, CELL), CELL)
        own = pl.ds(pl.multiple_of(slots + g * CELL, CELL), CELL)
        t = [sums[pl.ds(g * CELL * 16 + r, CELL, stride=16), :] * G_SCALE for r in range(12)]
        x = [xs[d, own, :] for d in range(3)]
        v = [pool2[d, own, :] for d in range(3)]
        mass = pool1[3, own, :]
        ratio = poolr[own, :]
        present = jnp.where(mass > 0, 1.0, 0.0)
        accel = [-(ratio * (x[d] * t[0] - t[1 + d]) + (x[d] * t[4] - t[5 + d])) for d in range(3)]
        heat = t[11]
        for d in range(3):
            heat = heat + x[d] * (v[d] * t[0] - t[8 + d]) - v[d] * t[1 + d]
        heat = ratio * heat
        speed = [v[d] + TIMESTEP * accel[d] for d in range(3)]
        place = [pool1[d, own, :] + TIMESTEP * speed[d] for d in range(3)]
        energy = pool2[3, own, :] + TIMESTEP * heat
        fields = place + speed + [mass, energy, pool1[4, own, :]] + [carried[f, at, :] for f in range(7)]
        for f, value in enumerate(fields):
            updated[pl.ds(g * CELL * FIELDS + f, CELL, stride=FIELDS), :] = value * present
        for f, value in enumerate([rho[at, :]] + accel + [heat]):
            derived[f, at, :] = value * present

    for copies in (waiting, second, third):
        for _, copy in copies:
            copy.wait_send()
    for copies in forwarded + passed:
        for copy in copies:
            copy.wait_send()
    for copy in r_copies:
        copy.wait_send()


def step(n_slab, n_tile, particles, dest_slot, neighbours, counts):
    slots = n_tile * CELL
    bins = particles.shape[0]
    dma = pltpu.SemaphoreType.DMA
    vmem = pl.BlockSpec(memory_space=pltpu.VMEM)
    updated, derived = pl.pallas_call(
        functools.partial(kernel, n_slab, n_tile),
        out_shape=(
            jax.ShapeDtypeStruct((slots * FIELDS, LANES), F32),
            jax.ShapeDtypeStruct((5, slots, LANES), F32),
        ),
        in_specs=[pl.BlockSpec(memory_space=pl.ANY)] * 4,
        out_specs=(vmem, vmem),
        scratch_shapes=[
            pltpu.SMEM((4, slots), jnp.int32),
            pltpu.SMEM((slots,), jnp.int32),
            pltpu.VMEM((1, bins), jnp.int32),
            pltpu.VMEM((bins * FIELDS, LANES), F32),
            pltpu.VMEM((FIELDS, slots, LANES), F32),
            pltpu.VMEM((5, 3 * slots, LANES), F32),
            pltpu.VMEM((4, 3 * slots, LANES), F32),
            pltpu.VMEM((7, slots, LANES), F32),
            pltpu.VMEM((3 * slots, LANES), F32),
            pltpu.VMEM((3, 3 * slots, LANES), F32),
            pltpu.VMEM((slots * ROWS, LANES), F32),
            pltpu.VMEM((3 * slots * ROWS, LANES), F32),
            pltpu.VMEM((3 * slots * ROWS, LANES), F32),
            pltpu.VMEM((3 * slots * ROWS, LANES), F32),
            pltpu.VMEM((slots * 4, LANES, LANES), F32),
            pltpu.VMEM((LANES, LANES), F32),
            pltpu.VMEM((slots * 16, LANES), F32),
            pltpu.VMEM((3 * slots, LANES), F32),
            pltpu.VMEM((slots // 4, LANES, LANES), BF16),
            pltpu.VMEM((4, LANES, 2 * LANES), F32),
            pltpu.VMEM((4, LANES, 2 * LANES), F32),
            pltpu.VMEM((LANES, LANES), F32),
            dma((4,)),
            dma((3, n_tile)),
            dma((3, n_tile)),
            dma((2, 2, n_tile)),
            dma((2, 2, n_tile)),
            dma((2, 2)),
            dma((2, 2)),
        ],
        compiler_params=pltpu.CompilerParams(collective_id=0, has_side_effects=True),
    )(neighbours.T, counts, dest_slot.reshape(1, bins), particles.reshape(bins * FIELDS, LANES))
    return updated.reshape(slots, FIELDS, LANES), derived.transpose(1, 0, 2)


def solution(mesh):
    in_specs = (
        P(("slab", "tile"), None, None),
        P(("slab", "tile")),
        P(("slab", "tile"), None),
        P(("slab", "tile")),
    )
    out_specs = (P(("slab", "tile"), None, None), P(("slab", "tile"), None, None))
    body = functools.partial(step, mesh.shape["slab"], mesh.shape["tile"])
    return jax.shard_map(body, mesh=mesh, in_specs=in_specs, out_specs=out_specs, check_vma=False)
```

```python
import functools
import math

import jax
import jax.numpy as jnp
from jax import lax
from jax.experimental import pallas as pl
from jax.experimental.pallas import tpu as pltpu
from jax.sharding import PartitionSpec as P

ADIABATIC = 5.0 / 3.0
TIMESTEP = 0.5
KERNEL_NORM = 21.0 / (16.0 * math.pi)
W_SCALE = KERNEL_NORM / 2048.0
G_SCALE = -160.0 * KERNEL_NORM / 65536.0

FIELDS = 16
CELL = 8
LANES = 128
ROWS = 32
ORDER = (0, 1, 2, 6, 8, 3, 4, 5, 7, 9, 10, 11, 12, 13, 14, 15)
GROUPS = ((0, 5), (5, 9), (9, 16))
F32 = jnp.float32
BF16 = jnp.bfloat16
MESH = pl.DeviceIdType.MESH


def halves(x, count):
    parts = []
    for _ in range(count - 1):
        part = x.astype(BF16).astype(F32)
        parts.append(part)
        x = x - part
    parts.append(x.astype(BF16).astype(F32))
    return parts


def kernel(
    n_slab,
    n_tile,
    nbr_in,
    cnt_in,
    dest_in,
    particles,
    updated,
    derived,
    nbr,
    cnt,
    dest,
    pbuf,
    outbox,
    pool1,
    pool2,
    carried,
    poolr,
    xs,
    self_rows,
    cand_d,
    cand_s,
    force_rows,
    slopes,
    rho,
    sums,
    masses,
    turned,
    even,
    odd,
    columns,
    in_sem,
    a2a_send,
    a2a_recv,
    halo_send,
    halo_recv,
    r_send,
    r_recv,
):
    slots = n_tile * CELL
    bins = pbuf.shape[0] // FIELDS
    groups = slots // CELL
    slab = lax.axis_index("slab")
    tile = lax.axis_index("tile")
    up = lax.rem(slab + 1, n_slab)
    down = lax.rem(slab + n_slab - 1, n_slab)

    barrier = pltpu.get_barrier_semaphore()
    for i in range(1, n_tile):
        peer = lax.rem(tile + i, n_tile)
        pl.semaphore_signal(barrier, inc=1, device_id=(slab, peer), device_id_type=MESH)
    for side in (up, down):
        pl.semaphore_signal(barrier, inc=1, device_id=(side, tile), device_id_type=MESH)

    loads = []
    for n, (source, target) in enumerate(((particles, pbuf), (dest_in, dest), (nbr_in, nbr), (cnt_in, cnt))):
        loads.append(pltpu.make_async_copy(source, target, in_sem.at[n]))
        loads[-1].start()

    zeros = jnp.zeros((CELL, LANES), F32)
    ones = jnp.ones((CELL, LANES), F32)
    depth = lax.broadcasted_iota(jnp.int32, (CELL, LANES), 0)

    def spread(ref, row):
        return (row // CELL) * (ref.shape[0] // 4)

    def constants():
        late = jnp.where(depth >= 4, 1.0, 0.0)
        early = jnp.where(depth < 2, 1.0, 0.0)
        middle = jnp.where((depth >= 2) & (depth < 5), 1.0, 0.0)
        fills = ((self_rows, slots, {1: late, 2: early, 3: zeros}),)
        fills += ((cand_d, 3 * slots, {1: late, 2: zeros, 3: zeros}),)
        fills += ((cand_s, 3 * slots, {0: zeros, 1: zeros, 2: middle, 3: zeros}),)
        fills += ((force_rows, 3 * slots, {1: zeros, 3: zeros}),)
        for ref, count, blocks in fills:

            @pl.loop(0, count // 8)
            def _(i):
                for r in range(8):
                    for kb, value in blocks.items():
                        ref[pl.ds(pl.multiple_of((kb * count + 8 * i + r) * CELL, CELL), CELL), :] = value

    loads[0].wait()
    loads[1].wait()

    cell = lax.broadcasted_iota(jnp.int32, (slots, bins), 0)
    hot = (cell == dest[...]).astype(BF16)
    hot = jnp.concatenate([hot, hot, hot], axis=1)

    def pack(lo, hi):
        for at in range(lo, hi):
            field = pbuf[pl.ds(ORDER[at], bins, stride=FIELDS), :]
            parts = jnp.concatenate([p.astype(BF16) for p in halves(field, 3)], axis=0)
            outbox[at] = jnp.dot(hot, parts, preferred_element_type=F32)

    mine = pl.ds(pl.multiple_of(tile * CELL, CELL), CELL)
    own_mine = pl.ds(pl.multiple_of(slots + tile * CELL, CELL), CELL)

    def landing(group, rows, own_rows):
        if group == 0:
            return pool1.at[:, own_rows, :]
        if group == 1:
            return pool2.at[:, own_rows, :]
        return carried.at[:, rows, :]

    def send(group):
        lo, hi = GROUPS[group]
        copies = []
        for i in sorted(range(1, n_tile), key=lambda j: min(j, n_tile - j)):
            peer = lax.rem(tile + i, n_tile)
            theirs = pl.ds(pl.multiple_of(peer * CELL, CELL), CELL)
            copy = pltpu.make_async_remote_copy(
                src_ref=outbox.at[lo:hi, theirs, :],
                dst_ref=landing(group, mine, own_mine),
                send_sem=a2a_send.at[group, i],
                recv_sem=a2a_recv.at[group, i],
                device_id=(slab, peer),
                device_id_type=MESH,
            )
            copy.start()
            copies.append((i, copy))
        pltpu.make_async_copy(
            outbox.at[lo:hi, mine, :], landing(group, mine, own_mine), a2a_recv.at[group, 0]
        ).start()
        return copies

    def settle(group):
        lo, hi = GROUPS[group]
        pltpu.make_async_copy(
            outbox.at[lo:hi, mine, :], landing(group, mine, own_mine), a2a_recv.at[group, 0]
        ).wait()

    def forward(kind, i):
        pool, fields = ((pool1, 5), (pool2, 3))[kind]
        source = lax.rem(tile + n_tile - i, n_tile) if i else tile
        copies = []
        for side, (target, base) in enumerate(((up, 0), (down, 2 * slots))):
            copy = pltpu.make_async_remote_copy(
                src_ref=pool.at[0:fields, pl.ds(pl.multiple_of(slots + source * CELL, CELL), CELL), :],
                dst_ref=pool.at[0:fields, pl.ds(pl.multiple_of(base + source * CELL, CELL), CELL), :],
                send_sem=halo_send.at[kind, side, i],
                recv_sem=halo_recv.at[kind, side, i],
                device_id=(target, tile),
                device_id_type=MESH,
            )
            copy.start()
            copies.append(copy)
        return copies

    def prepare(g, own):
        at = pl.ds(pl.multiple_of(g * CELL, CELL), CELL)
        mass = pool1[3, at, :]
        width = jnp.where(mass > 0, pool1[4, at, :], 1.0)
        masses[at, :] = mass
        q1, q2 = halves(0.25 * width, 2)
        q = q1 + q2
        norm = jnp.zeros((CELL, LANES), F32)

        def put(ref, row, value, group):
            ref[pl.ds(spread(ref, row) + group * CELL * CELL + row % CELL, CELL, stride=CELL), :] = value

        go = g - groups
        for d in range(3):
            x1, x2 = halves(pool1[d, at, :] - 1.0, 2)
            x = x1 + x2
            xs[d, at, :] = x
            norm = norm + x * x
            for r, (a, c) in enumerate(((x1, x1), (x1, x2), (x2, x1), (x2, x2))):
                put(cand_d, 4 * d + r, -2.0 * c, g)
                if own:
                    put(self_rows, 4 * d + r, a, go)
        for r, n in enumerate(halves(norm, 3)):
            put(cand_d, 15 + r, n, g)
            if own:
                put(self_rows, 12 + r, n, go)
        for r, n in enumerate(halves(q * q, 3)):
            put(cand_s, 15 + r, n, g)
            if own:
                put(self_rows, 18 + r, n, go)
        for r, (a, c) in enumerate(((q1, q1), (q1, q2), (q2, q1), (q2, q2))):
            put(cand_s, 21 + r, 2.0 * c, g)
            if own:
                put(self_rows, 21 + r, a, go)

    def slot_rows(ref, j):
        count = ref.shape[0] // 4
        return jnp.concatenate([ref[pl.ds(kb * count + j * CELL, CELL), :] for kb in range(4)], axis=0)

    def tile_rows(ref, j):
        return slot_rows(ref, j).astype(BF16)

    lane = lax.broadcasted_iota(jnp.int32, (ROWS, LANES), 1)

    def measure(buffer, t, block, r, j):
        far = jnp.concatenate([tile_rows(cand_d, j), tile_rows(cand_s, j)], axis=1)
        parts = [far]
        if r > 0:
            parts.insert(0, jnp.zeros((r * ROWS, 2 * LANES), BF16))
        if r < 3:
            parts.append(jnp.zeros(((3 - r) * ROWS, 2 * LANES), BF16))
        buffer[t] = jnp.dot(turned[block], jnp.concatenate(parts, axis=0), preferred_element_type=F32)

    def weigh(buffer, i, tiles):
        for at in range(0, LANES, ROWS):
            rows = slice(at, at + ROWS)
            w = None
            for t, place, mass in tiles:
                square = jnp.maximum(buffer[t, rows, 0:LANES], 1e-12)
                inv = lax.rsqrt(buffer[t, rows, LANES:])
                e = jnp.maximum(4.0 - (square * lax.rsqrt(square)) * inv, 0.0)
                h = e * inv
                g = (h * h) * h
                slope = g * (inv * inv)
                slopes[place, rows, :] = slope
                term = (g * (e * (5.0 - e))) * mass
                w = term if w is None else w + term
            column = jnp.sum(w, axis=1, keepdims=True)
            columns[rows, :] += jnp.where(lane == i, column, 0.0)

    def used(i, k):
        return lax.min(lax.max(cnt[i] - k, 0), 1).astype(F32)

    def offset_of(n):
        odd = lax.rem(n, 2)
        return odd * lax.div(n + 1, 2) + (1 - odd) * lax.rem(n_tile - lax.div(n, 2), n_tile)

    def source_of(n):
        return lax.rem(tile + n_tile - offset_of(n), n_tile)

    def self_measure(buffer, b):
        for r in range(4):
            measure(buffer, r, b, r, slots + 4 * b + r)

    def self_weigh(buffer, b):
        for r in range(4):
            i = 4 * b + r
            weigh(buffer, i, [(r, 4 * i, masses[slots + i][None, :])])

    def against_self(lo, hi):
        @pl.loop(lo, hi)
        def _(n):
            source = source_of(n)
            prepare(source + groups, True)

        @pl.loop(lo, hi)
        def _(n):
            for h in range(2):
                b = 2 * source_of(n) + h
                rows = [slot_rows(self_rows, 4 * b + r) for r in range(4)]
                turned[b] = jnp.concatenate(rows, axis=0).T.astype(BF16)

        self_measure(even, 2 * source_of(jnp.int32(lo)))

        @pl.loop(lo, hi)
        def _(n):
            b = 2 * source_of(n)
            self_measure(odd, b + 1)
            self_weigh(even, b)
            self_measure(even, 2 * source_of(lax.min(n + 1, hi - 1)))
            self_weigh(odd, b + 1)

    pack(*GROUPS[0])
    pl.semaphore_wait(barrier, n_tile + 1)
    waiting = send(0)
    by_offset = dict(waiting)
    columns[...] = jnp.zeros((LANES, LANES), F32)
    constants()
    pack(*GROUPS[1])
    pack(*GROUPS[2])
    settle(0)
    forwarded = [forward(0, 0)]
    second = []
    cuts = sorted({min(c, n_tile) for c in (0, 3, 5, 8)} | {n_tile})
    for lo, hi in zip(cuts[:-1], cuts[1:]):
        for n in range(max(lo, 1), hi):
            i = (n + 1) // 2 if n % 2 else n_tile - n // 2
            by_offset[i].wait_recv()
            forwarded.append(forward(0, i))
        if hi == n_tile:
            second = send(1)
        against_self(lo, hi)

    for copies in forwarded:
        for copy in copies:
            copy.wait_recv()

    @pl.loop(0, groups)
    def _(g):
        prepare(g, False)
        prepare(g + 2 * groups, False)

    for load in loads[2:]:
        load.wait()

    chunk = slots // 2

    def others_measure(buffer, b, r):
        for k in range(1, 4):
            measure(buffer, k - 1, b, r, nbr[k, 4 * b + r])

    def others_weigh(buffer, b, r):
        i = 4 * b + r
        tiles = []
        for k in range(1, 4):
            tiles.append((k - 1, 4 * i + k, masses[nbr[k, i]][None, :] * used(i, k)))
        weigh(buffer, i, tiles)

    def ratio_copies(c):
        rows = c * chunk
        return [
            pltpu.make_async_remote_copy(
                src_ref=poolr.at[pl.ds(slots + rows, chunk), :],
                dst_ref=poolr.at[pl.ds(base + rows, chunk), :],
                send_sem=r_send.at[side, c],
                recv_sem=r_recv.at[side, c],
                device_id=(target, tile),
                device_id_type=MESH,
            )
            for side, (target, base) in enumerate(((up, 0), (down, 2 * slots)))
        ]

    others_measure(even, 0, 0)
    for c in range(2):
        @pl.loop(0, chunk // 4)
        def _(p):
            b = c * (chunk // 4) + p
            for r in range(4):
                ahead, now = (odd, even) if r % 2 == 0 else (even, odd)
                if r < 3:
                    others_measure(ahead, b, r + 1)
                else:
                    others_measure(ahead, lax.min(b + 1, slots // 4 - 1), 0)
                others_weigh(now, b, r)

        if c == 0:
            settle(1)
            for _, copy in second:
                copy.wait_recv()
            passed = [forward(1, i) for i in range(n_tile)]
            third = send(2)

        rho[...] = columns[...].T * W_SCALE

        @pl.loop(0, chunk // CELL)
        def _(p):
            row = pl.multiple_of(c * chunk + p * CELL, CELL)
            at = pl.ds(slots + row, CELL)
            density = rho[pl.ds(row, CELL), :]
            pressure = (ADIABATIC - 1.0) * density * pool2[3, at, :]
            safe = jnp.where(pool1[3, at, :] > 0, density, 1.0)
            poolr[at, :] = pressure / (safe * safe)

        for copy in ratio_copies(c):
            copy.start()

    r_copies = ratio_copies(0) + ratio_copies(1)

    for copies in passed:
        for copy in copies:
            copy.wait_recv()

    def put_force(row, g, value):
        high, low = halves(value, 2)
        for base, part in ((row, high), (row + 16, low)):
            at = pl.ds(spread(force_rows, base) + g * CELL * CELL + base % CELL, CELL, stride=CELL)
            force_rows[at, :] = part

    def prepare_motion(g):
        at = pl.ds(pl.multiple_of(g * CELL, CELL), CELL)
        mass = pool1[3, at, :]
        x = [xs[d, at, :] for d in range(3)]
        v = [pool2[d, at, :] for d in range(3)]
        put_force(0, g, mass)
        for d in range(3):
            put_force(1 + d, g, mass * x[d])
            put_force(8 + d, g, mass * v[d])
        put_force(11, g, mass * (x[0] * v[0] + x[1] * v[1] + x[2] * v[2]))

    def prepare_ratio(g):
        at = pl.ds(pl.multiple_of(g * CELL, CELL), CELL)
        massed = pool1[3, at, :] * poolr[at, :]
        put_force(4, g, massed)
        for d in range(3):
            put_force(5 + d, g, massed * xs[d, at, :])

    def pull(tiles):
        lefts, rights = [], []
        for j, place, weight in tiles:
            rows = (slot_rows(force_rows, j) * weight).astype(BF16)
            slope = slopes[place]
            high = slope.astype(BF16)
            lefts += [rows, rows]
            rights += [high, (slope - high.astype(F32)).astype(BF16)]
        out = lax.dot_general(
            jnp.concatenate(lefts, axis=1),
            jnp.concatenate(rights, axis=1),
            (((1,), (1,)), ((), ())),
            preferred_element_type=F32,
        )
        return out[0:16] + out[16:32]

    @pl.loop(0, groups)
    def _(g):
        prepare_motion(g + groups)
        prepare_ratio(g + groups)

    @pl.loop(0, slots // 16)
    def _(b):
        for r in range(16):
            i = 16 * b + r
            sums[pl.ds(pl.multiple_of(i * 16, 16), 16), :] = pull([(slots + i, 4 * i, 1.0)])

    @pl.loop(0, groups)
    def _(g):
        prepare_motion(g)
        prepare_motion(g + 2 * groups)

    for copy in r_copies:
        copy.wait_recv()

    @pl.loop(0, groups)
    def _(g):
        prepare_ratio(g)
        prepare_ratio(g + 2 * groups)

    @pl.loop(0, slots // 16)
    def _(b):
        for r in range(16):
            i = 16 * b + r
            tiles = [(nbr[k, i], 4 * i + k, used(i, k)) for k in range(1, 4)]
            sums[pl.ds(pl.multiple_of(i * 16, 16), 16), :] += pull(tiles)

    settle(2)
    for _, copy in third:
        copy.wait_recv()

    @pl.loop(0, groups)
    def _(g):
        at = pl.ds(pl.multiple_of(g * CELL, CELL), CELL)
        own = pl.ds(pl.multiple_of(slots + g * CELL, CELL), CELL)
        t = [sums[pl.ds(g * CELL * 16 + r, CELL, stride=16), :] * G_SCALE for r in range(12)]
        x = [xs[d, own, :] for d in range(3)]
        v = [pool2[d, own, :] for d in range(3)]
        mass = pool1[3, own, :]
        ratio = poolr[own, :]
        present = jnp.where(mass > 0, 1.0, 0.0)
        accel = [-(ratio * (x[d] * t[0] - t[1 + d]) + (x[d] * t[4] - t[5 + d])) for d in range(3)]
        heat = t[11]
        for d in range(3):
            heat = heat + x[d] * (v[d] * t[0] - t[8 + d]) - v[d] * t[1 + d]
        heat = ratio * heat
        speed = [v[d] + TIMESTEP * accel[d] for d in range(3)]
        place = [pool1[d, own, :] + TIMESTEP * speed[d] for d in range(3)]
        energy = pool2[3, own, :] + TIMESTEP * heat
        fields = place + speed + [mass, energy, pool1[4, own, :]] + [carried[f, at, :] for f in range(7)]
        for f, value in enumerate(fields):
            updated[pl.ds(g * CELL * FIELDS + f, CELL, stride=FIELDS), :] = value * present
        for f, value in enumerate([rho[at, :]] + accel + [heat]):
            derived[f, at, :] = value * present

    for copies in (waiting, second, third):
        for _, copy in copies:
            copy.wait_send()
    for copies in forwarded + passed:
        for copy in copies:
            copy.wait_send()
    for copy in r_copies:
        copy.wait_send()


def step(n_slab, n_tile, particles, dest_slot, neighbours, counts):
    slots = n_tile * CELL
    bins = particles.shape[0]
    dma = pltpu.SemaphoreType.DMA
    vmem = pl.BlockSpec(memory_space=pltpu.VMEM)
    updated, derived = pl.pallas_call(
        functools.partial(kernel, n_slab, n_tile),
        out_shape=(
            jax.ShapeDtypeStruct((slots * FIELDS, LANES), F32),
            jax.ShapeDtypeStruct((5, slots, LANES), F32),
        ),
        in_specs=[pl.BlockSpec(memory_space=pl.ANY)] * 4,
        out_specs=(vmem, vmem),
        scratch_shapes=[
            pltpu.SMEM((4, slots), jnp.int32),
            pltpu.SMEM((slots,), jnp.int32),
            pltpu.VMEM((1, bins), jnp.int32),
            pltpu.VMEM((bins * FIELDS, LANES), F32),
            pltpu.VMEM((FIELDS, slots, LANES), F32),
            pltpu.VMEM((5, 3 * slots, LANES), F32),
            pltpu.VMEM((4, 3 * slots, LANES), F32),
            pltpu.VMEM((7, slots, LANES), F32),
            pltpu.VMEM((3 * slots, LANES), F32),
            pltpu.VMEM((3, 3 * slots, LANES), F32),
            pltpu.VMEM((slots * ROWS, LANES), F32),
            pltpu.VMEM((3 * slots * ROWS, LANES), F32),
            pltpu.VMEM((3 * slots * ROWS, LANES), F32),
            pltpu.VMEM((3 * slots * ROWS, LANES), F32),
            pltpu.VMEM((slots * 4, LANES, LANES), F32),
            pltpu.VMEM((LANES, LANES), F32),
            pltpu.VMEM((slots * 16, LANES), F32),
            pltpu.VMEM((3 * slots, LANES), F32),
            pltpu.VMEM((slots // 4, LANES, LANES), BF16),
            pltpu.VMEM((4, LANES, 2 * LANES), F32),
            pltpu.VMEM((4, LANES, 2 * LANES), F32),
            pltpu.VMEM((LANES, LANES), F32),
            dma((4,)),
            dma((3, n_tile)),
            dma((3, n_tile)),
            dma((2, 2, n_tile)),
            dma((2, 2, n_tile)),
            dma((2, 2)),
            dma((2, 2)),
        ],
        compiler_params=pltpu.CompilerParams(collective_id=0, has_side_effects=True),
    )(neighbours.T, counts, dest_slot.reshape(1, bins), particles.reshape(bins * FIELDS, LANES))
    return updated.reshape(slots, FIELDS, LANES), derived.transpose(1, 0, 2)


def solution(mesh):
    in_specs = (
        P(("slab", "tile"), None, None),
        P(("slab", "tile")),
        P(("slab", "tile"), None),
        P(("slab", "tile")),
    )
    out_specs = (P(("slab", "tile"), None, None), P(("slab", "tile"), None, None))
    body = functools.partial(step, mesh.shape["slab"], mesh.shape["tile"])
    return jax.shard_map(body, mesh=mesh, in_specs=in_specs, out_specs=out_specs, check_vma=False)
```

```python
import functools
import math

import jax
import jax.numpy as jnp
from jax import lax
from jax.experimental import pallas as pl
from jax.experimental.pallas import tpu as pltpu
from jax.sharding import PartitionSpec as P

ADIABATIC = 5.0 / 3.0
TIMESTEP = 0.5
KERNEL_NORM = 21.0 / (16.0 * math.pi)
W_SCALE = KERNEL_NORM / 2048.0
G_SCALE = -160.0 * KERNEL_NORM / 65536.0

FIELDS = 16
VMEM_BYTES = 52000 * 1024
CELL = 8
LANES = 128
ROWS = 32
ORDER = (0, 1, 2, 6, 8, 3, 4, 5, 7, 9, 10, 11, 12, 13, 14, 15)
GROUPS = ((0, 5), (5, 9), (9, 16))
F32 = jnp.float32
BF16 = jnp.bfloat16
MESH = pl.DeviceIdType.MESH


def halves(x, count):
    parts = []
    for _ in range(count - 1):
        part = x.astype(BF16).astype(F32)
        parts.append(part)
        x = x - part
    parts.append(x.astype(BF16).astype(F32))
    return parts


def kernel(
    n_slab,
    n_tile,
    nbr_in,
    cnt_in,
    dest_in,
    particles,
    updated,
    derived,
    nbr,
    cnt,
    dest,
    pbuf,
    outbox,
    pool1,
    pool2,
    carried,
    poolr,
    xs,
    self_rows,
    cand_d,
    cand_s,
    force_rows,
    slopes,
    rho,
    sums,
    masses,
    turned,
    even,
    odd,
    columns,
    in_sem,
    a2a_send,
    a2a_recv,
    halo_send,
    halo_recv,
    r_send,
    r_recv,
):
    slots = n_tile * CELL
    bins = pbuf.shape[0] // FIELDS
    groups = slots // CELL
    slab = lax.axis_index("slab")
    tile = lax.axis_index("tile")
    up = lax.rem(slab + 1, n_slab)
    down = lax.rem(slab + n_slab - 1, n_slab)

    barrier = pltpu.get_barrier_semaphore()
    for i in range(1, n_tile):
        peer = lax.rem(tile + i, n_tile)
        pl.semaphore_signal(barrier, inc=1, device_id=(slab, peer), device_id_type=MESH)
    for side in (up, down):
        pl.semaphore_signal(barrier, inc=1, device_id=(side, tile), device_id_type=MESH)

    loads = []
    for n, (source, target) in enumerate(((particles, pbuf), (dest_in, dest), (nbr_in, nbr), (cnt_in, cnt))):
        loads.append(pltpu.make_async_copy(source, target, in_sem.at[n]))
        loads[-1].start()

    zeros = jnp.zeros((CELL, LANES), F32)
    ones = jnp.ones((CELL, LANES), F32)
    depth = lax.broadcasted_iota(jnp.int32, (CELL, LANES), 0)

    def spread(ref, row):
        return (row // CELL) * (ref.shape[0] // 4)

    def constants():
        late = jnp.where(depth >= 4, 1.0, 0.0)
        early = jnp.where(depth < 2, 1.0, 0.0)
        middle = jnp.where((depth >= 2) & (depth < 5), 1.0, 0.0)
        fills = ((self_rows, slots, {1: late, 2: early, 3: zeros}),)
        fills += ((cand_d, 3 * slots, {1: late, 2: zeros, 3: zeros}),)
        fills += ((cand_s, 3 * slots, {0: zeros, 1: zeros, 2: middle, 3: zeros}),)
        fills += ((force_rows, 3 * slots, {1: zeros, 3: zeros}),)
        for ref, count, blocks in fills:

            @pl.loop(0, count // 8)
            def _(i):
                for r in range(8):
                    for kb, value in blocks.items():
                        ref[pl.ds(pl.multiple_of((kb * count + 8 * i + r) * CELL, CELL), CELL), :] = value

    loads[0].wait()
    loads[1].wait()

    cell = lax.broadcasted_iota(jnp.int32, (slots, bins), 0)
    hot = (cell == dest[...]).astype(BF16)
    hot = jnp.concatenate([hot, hot, hot], axis=1)

    def pack(lo, hi):
        for at in range(lo, hi):
            field = pbuf[pl.ds(ORDER[at], bins, stride=FIELDS), :]
            parts = jnp.concatenate([p.astype(BF16) for p in halves(field, 3)], axis=0)
            outbox[at] = jnp.dot(hot, parts, preferred_element_type=F32)

    mine = pl.ds(pl.multiple_of(tile * CELL, CELL), CELL)
    own_mine = pl.ds(pl.multiple_of(slots + tile * CELL, CELL), CELL)

    def landing(group, rows, own_rows):
        if group == 0:
            return pool1.at[:, own_rows, :]
        if group == 1:
            return pool2.at[:, own_rows, :]
        return carried.at[:, rows, :]

    def send(group):
        lo, hi = GROUPS[group]
        copies = []
        for i in sorted(range(1, n_tile), key=lambda j: min(j, n_tile - j)):
            peer = lax.rem(tile + i, n_tile)
            theirs = pl.ds(pl.multiple_of(peer * CELL, CELL), CELL)
            copy = pltpu.make_async_remote_copy(
                src_ref=outbox.at[lo:hi, theirs, :],
                dst_ref=landing(group, mine, own_mine),
                send_sem=a2a_send.at[group, i],
                recv_sem=a2a_recv.at[group, i],
                device_id=(slab, peer),
                device_id_type=MESH,
            )
            copy.start()
            copies.append((i, copy))
        pltpu.make_async_copy(
            outbox.at[lo:hi, mine, :], landing(group, mine, own_mine), a2a_recv.at[group, 0]
        ).start()
        return copies

    def settle(group):
        lo, hi = GROUPS[group]
        pltpu.make_async_copy(
            outbox.at[lo:hi, mine, :], landing(group, mine, own_mine), a2a_recv.at[group, 0]
        ).wait()

    def forward(kind, i):
        pool, fields = ((pool1, 5), (pool2, 3))[kind]
        source = lax.rem(tile + n_tile - i, n_tile) if i else tile
        copies = []
        for side, (target, base) in enumerate(((up, 0), (down, 2 * slots))):
            copy = pltpu.make_async_remote_copy(
                src_ref=pool.at[0:fields, pl.ds(pl.multiple_of(slots + source * CELL, CELL), CELL), :],
                dst_ref=pool.at[0:fields, pl.ds(pl.multiple_of(base + source * CELL, CELL), CELL), :],
                send_sem=halo_send.at[kind, side, i],
                recv_sem=halo_recv.at[kind, side, i],
                device_id=(target, tile),
                device_id_type=MESH,
            )
            copy.start()
            copies.append(copy)
        return copies

    def prepare(g, own):
        at = pl.ds(pl.multiple_of(g * CELL, CELL), CELL)
        mass = pool1[3, at, :]
        width = jnp.where(mass > 0, pool1[4, at, :], 1.0)
        masses[at, :] = mass
        q1, q2 = halves(0.25 * width, 2)
        q = q1 + q2
        norm = jnp.zeros((CELL, LANES), F32)

        def put(ref, row, value, group):
            ref[pl.ds(spread(ref, row) + group * CELL * CELL + row % CELL, CELL, stride=CELL), :] = value

        go = g - groups
        for d in range(3):
            x1, x2 = halves(pool1[d, at, :] - 1.0, 2)
            x = x1 + x2
            xs[d, at, :] = x
            norm = norm + x * x
            for r, (a, c) in enumerate(((x1, x1), (x1, x2), (x2, x1), (x2, x2))):
                put(cand_d, 4 * d + r, -2.0 * c, g)
                if own:
                    put(self_rows, 4 * d + r, a, go)
        for r, n in enumerate(halves(norm, 3)):
            put(cand_d, 15 + r, n, g)
            if own:
                put(self_rows, 12 + r, n, go)
        for r, n in enumerate(halves(q * q, 3)):
            put(cand_s, 15 + r, n, g)
            if own:
                put(self_rows, 18 + r, n, go)
        for r, (a, c) in enumerate(((q1, q1), (q1, q2), (q2, q1), (q2, q2))):
            put(cand_s, 21 + r, 2.0 * c, g)
            if own:
                put(self_rows, 21 + r, a, go)

    def slot_rows(ref, j):
        count = ref.shape[0] // 4
        return jnp.concatenate([ref[pl.ds(kb * count + j * CELL, CELL), :] for kb in range(4)], axis=0)

    def tile_rows(ref, j):
        return slot_rows(ref, j).astype(BF16)

    lane = lax.broadcasted_iota(jnp.int32, (ROWS, LANES), 1)

    def measure(buffer, t, block, r, j):
        far = jnp.concatenate([tile_rows(cand_d, j), tile_rows(cand_s, j)], axis=1)
        parts = [far]
        if r > 0:
            parts.insert(0, jnp.zeros((r * ROWS, 2 * LANES), BF16))
        if r < 3:
            parts.append(jnp.zeros(((3 - r) * ROWS, 2 * LANES), BF16))
        buffer[t] = jnp.dot(turned[block], jnp.concatenate(parts, axis=0), preferred_element_type=F32)

    def weigh(buffer, i, tiles):
        for at in range(0, LANES, ROWS):
            rows = slice(at, at + ROWS)
            w = None
            for t, place, mass in tiles:
                square = jnp.maximum(buffer[t, rows, 0:LANES], 1e-12)
                inv = lax.rsqrt(buffer[t, rows, LANES:])
                e = jnp.maximum(4.0 - (square * lax.rsqrt(square)) * inv, 0.0)
                h = e * inv
                g = (h * h) * h
                slope = g * (inv * inv)
                slopes[place, rows, :] = slope
                term = (g * (e * (5.0 - e))) * mass
                w = term if w is None else w + term
            column = jnp.sum(w, axis=1, keepdims=True)
            columns[rows, :] += jnp.where(lane == i, column, 0.0)

    def used(i, k):
        return lax.min(lax.max(cnt[i] - k, 0), 1).astype(F32)

    def offset_of(n):
        odd = lax.rem(n, 2)
        return odd * lax.div(n + 1, 2) + (1 - odd) * lax.rem(n_tile - lax.div(n, 2), n_tile)

    def source_of(n):
        return lax.rem(tile + n_tile - offset_of(n), n_tile)

    def self_measure(buffer, b):
        for r in range(4):
            measure(buffer, r, b, r, slots + 4 * b + r)

    def self_weigh(buffer, b):
        for r in range(4):
            i = 4 * b + r
            weigh(buffer, i, [(r, 4 * i, masses[slots + i][None, :])])

    def against_self(lo, hi):
        @pl.loop(lo, hi)
        def _(n):
            source = source_of(n)
            prepare(source + groups, True)

        @pl.loop(lo, hi)
        def _(n):
            for h in range(2):
                b = 2 * source_of(n) + h
                rows = [slot_rows(self_rows, 4 * b + r) for r in range(4)]
                turned[b] = jnp.concatenate(rows, axis=0).T.astype(BF16)

        self_measure(even, 2 * source_of(jnp.int32(lo)))

        @pl.loop(lo, hi)
        def _(n):
            b = 2 * source_of(n)
            self_measure(odd, b + 1)
            self_weigh(even, b)
            self_measure(even, 2 * source_of(lax.min(n + 1, hi - 1)))
            self_weigh(odd, b + 1)

    pack(*GROUPS[0])
    pl.semaphore_wait(barrier, n_tile + 1)
    waiting = send(0)
    by_offset = dict(waiting)
    columns[...] = jnp.zeros((LANES, LANES), F32)
    constants()
    pack(*GROUPS[1])
    pack(*GROUPS[2])
    settle(0)
    forwarded = [forward(0, 0)]
    second = []
    cuts = sorted({min(c, n_tile) for c in (0, 3, 5, 8)} | {n_tile})
    for lo, hi in zip(cuts[:-1], cuts[1:]):
        for n in range(max(lo, 1), hi):
            i = (n + 1) // 2 if n % 2 else n_tile - n // 2
            by_offset[i].wait_recv()
            forwarded.append(forward(0, i))
        if hi == n_tile:
            second = send(1)
        against_self(lo, hi)

    for copies in forwarded:
        for copy in copies:
            copy.wait_recv()

    @pl.loop(0, groups)
    def _(g):
        prepare(g, False)
        prepare(g + 2 * groups, False)

    for load in loads[2:]:
        load.wait()

    chunk = slots // 2

    def others_measure(buffer, b, r):
        for k in range(1, 4):
            measure(buffer, k - 1, b, r, nbr[k, 4 * b + r])

    def others_weigh(buffer, b, r):
        i = 4 * b + r
        tiles = []
        for k in range(1, 4):
            tiles.append((k - 1, 4 * i + k, masses[nbr[k, i]][None, :] * used(i, k)))
        weigh(buffer, i, tiles)

    def ratio_copies(c):
        rows = c * chunk
        return [
            pltpu.make_async_remote_copy(
                src_ref=poolr.at[pl.ds(slots + rows, chunk), :],
                dst_ref=poolr.at[pl.ds(base + rows, chunk), :],
                send_sem=r_send.at[side, c],
                recv_sem=r_recv.at[side, c],
                device_id=(target, tile),
                device_id_type=MESH,
            )
            for side, (target, base) in enumerate(((up, 0), (down, 2 * slots)))
        ]

    others_measure(even, 0, 0)
    for c in range(2):
        @pl.loop(0, chunk // 4)
        def _(p):
            b = c * (chunk // 4) + p
            for r in range(4):
                ahead, now = (odd, even) if r % 2 == 0 else (even, odd)
                if r < 3:
                    others_measure(ahead, b, r + 1)
                else:
                    others_measure(ahead, lax.min(b + 1, slots // 4 - 1), 0)
                others_weigh(now, b, r)

        if c == 0:
            settle(1)
            for _, copy in second:
                copy.wait_recv()
            passed = [forward(1, i) for i in range(n_tile)]
            third = send(2)

        rho[...] = columns[...].T * W_SCALE

        @pl.loop(0, chunk // CELL)
        def _(p):
            row = pl.multiple_of(c * chunk + p * CELL, CELL)
            at = pl.ds(slots + row, CELL)
            density = rho[pl.ds(row, CELL), :]
            pressure = (ADIABATIC - 1.0) * density * pool2[3, at, :]
            safe = jnp.where(pool1[3, at, :] > 0, density, 1.0)
            poolr[at, :] = pressure / (safe * safe)

        for copy in ratio_copies(c):
            copy.start()

    r_copies = ratio_copies(0) + ratio_copies(1)

    for copies in passed:
        for copy in copies:
            copy.wait_recv()

    def put_force(row, g, value):
        high, low = halves(value, 2)
        for base, part in ((row, high), (row + 16, low)):
            at = pl.ds(spread(force_rows, base) + g * CELL * CELL + base % CELL, CELL, stride=CELL)
            force_rows[at, :] = part

    def prepare_motion(g):
        at = pl.ds(pl.multiple_of(g * CELL, CELL), CELL)
        mass = pool1[3, at, :]
        x = [xs[d, at, :] for d in range(3)]
        v = [pool2[d, at, :] for d in range(3)]
        put_force(0, g, mass)
        for d in range(3):
            put_force(1 + d, g, mass * x[d])
            put_force(8 + d, g, mass * v[d])
        put_force(11, g, mass * (x[0] * v[0] + x[1] * v[1] + x[2] * v[2]))

    def prepare_ratio(g):
        at = pl.ds(pl.multiple_of(g * CELL, CELL), CELL)
        massed = pool1[3, at, :] * poolr[at, :]
        put_force(4, g, massed)
        for d in range(3):
            put_force(5 + d, g, massed * xs[d, at, :])

    def pull(tiles):
        lefts, rights = [], []
        for j, place, weight in tiles:
            rows = (slot_rows(force_rows, j) * weight).astype(BF16)
            slope = slopes[place]
            high = slope.astype(BF16)
            lefts += [rows, rows]
            rights += [high, (slope - high.astype(F32)).astype(BF16)]
        out = lax.dot_general(
            jnp.concatenate(lefts, axis=1),
            jnp.concatenate(rights, axis=1),
            (((1,), (1,)), ((), ())),
            preferred_element_type=F32,
        )
        return out[0:16] + out[16:32]

    @pl.loop(0, groups)
    def _(g):
        prepare_motion(g + groups)
        prepare_ratio(g + groups)

    @pl.loop(0, slots // 16)
    def _(b):
        for r in range(16):
            i = 16 * b + r
            sums[pl.ds(pl.multiple_of(i * 16, 16), 16), :] = pull([(slots + i, 4 * i, 1.0)])

    @pl.loop(0, groups)
    def _(g):
        prepare_motion(g)
        prepare_motion(g + 2 * groups)

    for copy in r_copies:
        copy.wait_recv()

    @pl.loop(0, groups)
    def _(g):
        prepare_ratio(g)
        prepare_ratio(g + 2 * groups)

    @pl.loop(0, slots // 16)
    def _(b):
        for r in range(16):
            i = 16 * b + r
            tiles = [(nbr[k, i], 4 * i + k, used(i, k)) for k in range(1, 4)]
            sums[pl.ds(pl.multiple_of(i * 16, 16), 16), :] += pull(tiles)

    settle(2)
    for _, copy in third:
        copy.wait_recv()

    @pl.loop(0, groups)
    def _(g):
        at = pl.ds(pl.multiple_of(g * CELL, CELL), CELL)
        own = pl.ds(pl.multiple_of(slots + g * CELL, CELL), CELL)
        t = [sums[pl.ds(g * CELL * 16 + r, CELL, stride=16), :] * G_SCALE for r in range(12)]
        x = [xs[d, own, :] for d in range(3)]
        v = [pool2[d, own, :] for d in range(3)]
        mass = pool1[3, own, :]
        ratio = poolr[own, :]
        present = jnp.where(mass > 0, 1.0, 0.0)
        accel = [-(ratio * (x[d] * t[0] - t[1 + d]) + (x[d] * t[4] - t[5 + d])) for d in range(3)]
        heat = t[11]
        for d in range(3):
            heat = heat + x[d] * (v[d] * t[0] - t[8 + d]) - v[d] * t[1 + d]
        heat = ratio * heat
        speed = [v[d] + TIMESTEP * accel[d] for d in range(3)]
        place = [pool1[d, own, :] + TIMESTEP * speed[d] for d in range(3)]
        energy = pool2[3, own, :] + TIMESTEP * heat
        fields = place + speed + [mass, energy, pool1[4, own, :]] + [carried[f, at, :] for f in range(7)]
        for f, value in enumerate(fields):
            updated[pl.ds(g * CELL * FIELDS + f, CELL, stride=FIELDS), :] = value * present
        for f, value in enumerate([rho[at, :]] + accel + [heat]):
            derived[f, at, :] = value * present

    for copies in (waiting, second, third):
        for _, copy in copies:
            copy.wait_send()
    for copies in forwarded + passed:
        for copy in copies:
            copy.wait_send()
    for copy in r_copies:
        copy.wait_send()


def step(n_slab, n_tile, particles, dest_slot, neighbours, counts):
    slots = n_tile * CELL
    bins = particles.shape[0]
    dma = pltpu.SemaphoreType.DMA
    vmem = pl.BlockSpec(memory_space=pltpu.VMEM)
    updated, derived = pl.pallas_call(
        functools.partial(kernel, n_slab, n_tile),
        out_shape=(
            jax.ShapeDtypeStruct((slots * FIELDS, LANES), F32),
            jax.ShapeDtypeStruct((5, slots, LANES), F32),
        ),
        in_specs=[pl.BlockSpec(memory_space=pl.ANY)] * 4,
        out_specs=(vmem, vmem),
        scratch_shapes=[
            pltpu.SMEM((4, slots), jnp.int32),
            pltpu.SMEM((slots,), jnp.int32),
            pltpu.VMEM((1, bins), jnp.int32),
            pltpu.VMEM((bins * FIELDS, LANES), F32),
            pltpu.VMEM((FIELDS, slots, LANES), F32),
            pltpu.VMEM((5, 3 * slots, LANES), F32),
            pltpu.VMEM((4, 3 * slots, LANES), F32),
            pltpu.VMEM((7, slots, LANES), F32),
            pltpu.VMEM((3 * slots, LANES), F32),
            pltpu.VMEM((3, 3 * slots, LANES), F32),
            pltpu.VMEM((slots * ROWS, LANES), F32),
            pltpu.VMEM((3 * slots * ROWS, LANES), F32),
            pltpu.VMEM((3 * slots * ROWS, LANES), F32),
            pltpu.VMEM((3 * slots * ROWS, LANES), F32),
            pltpu.VMEM((slots * 4, LANES, LANES), F32),
            pltpu.VMEM((LANES, LANES), F32),
            pltpu.VMEM((slots * 16, LANES), F32),
            pltpu.VMEM((3 * slots, LANES), F32),
            pltpu.VMEM((slots // 4, LANES, LANES), BF16),
            pltpu.VMEM((4, LANES, 2 * LANES), F32),
            pltpu.VMEM((4, LANES, 2 * LANES), F32),
            pltpu.VMEM((LANES, LANES), F32),
            dma((4,)),
            dma((3, n_tile)),
            dma((3, n_tile)),
            dma((2, 2, n_tile)),
            dma((2, 2, n_tile)),
            dma((2, 2)),
            dma((2, 2)),
        ],
        compiler_params=pltpu.CompilerParams(collective_id=0, has_side_effects=True, vmem_limit_bytes=VMEM_BYTES),
    )(*(
        pltpu.with_memory_space_constraint(x, pltpu.HBM)
        for x in (neighbours.T, counts, dest_slot.reshape(1, bins), particles.reshape(bins * FIELDS, LANES))
    ))
    return updated.reshape(slots, FIELDS, LANES), derived.transpose(1, 0, 2)


def solution(mesh):
    in_specs = (
        P(("slab", "tile"), None, None),
        P(("slab", "tile")),
        P(("slab", "tile"), None),
        P(("slab", "tile")),
    )
    out_specs = (P(("slab", "tile"), None, None), P(("slab", "tile"), None, None))
    body = functools.partial(step, mesh.shape["slab"], mesh.shape["tile"])
    return jax.shard_map(body, mesh=mesh, in_specs=in_specs, out_specs=out_specs, check_vma=False)
```

```python
import functools
import math

import jax
import jax.numpy as jnp
from jax import lax
from jax.experimental import pallas as pl
from jax.experimental.pallas import tpu as pltpu
from jax.sharding import PartitionSpec as P

ADIABATIC = 5.0 / 3.0
TIMESTEP = 0.5
KERNEL_NORM = 21.0 / (16.0 * math.pi)
W_SCALE = KERNEL_NORM / 2048.0
G_SCALE = -160.0 * KERNEL_NORM / 65536.0

FIELDS = 16
VMEM_BYTES = 52000 * 1024
CELL = 8
LANES = 128
ROWS = 32
ORDER = (0, 1, 2, 6, 8, 3, 4, 5, 7, 9, 10, 11, 12, 13, 14, 15)
GROUPS = ((0, 5), (5, 9), (9, 16))
F32 = jnp.float32
BF16 = jnp.bfloat16
MESH = pl.DeviceIdType.MESH


def halves(x, count):
    parts = []
    for _ in range(count - 1):
        part = x.astype(BF16).astype(F32)
        parts.append(part)
        x = x - part
    parts.append(x.astype(BF16).astype(F32))
    return parts


def kernel(
    n_slab,
    n_tile,
    nbr_in,
    cnt_in,
    dest_in,
    particles,
    updated,
    derived,
    nbr,
    cnt,
    dest,
    pbuf,
    outbox,
    pool1,
    pool2,
    carried,
    poolr,
    xs,
    self_rows,
    cand_d,
    cand_s,
    force_rows,
    slopes,
    rho,
    sums,
    masses,
    turned,
    even,
    odd,
    columns,
    in_sem,
    a2a_send,
    a2a_recv,
    halo_send,
    halo_recv,
    r_send,
    r_recv,
):
    slots = n_tile * CELL
    bins = pbuf.shape[0] // FIELDS
    groups = slots // CELL
    slab = lax.axis_index("slab")
    tile = lax.axis_index("tile")
    up = lax.rem(slab + 1, n_slab)
    down = lax.rem(slab + n_slab - 1, n_slab)

    barrier = pltpu.get_barrier_semaphore()
    for i in range(1, n_tile):
        peer = lax.rem(tile + i, n_tile)
        pl.semaphore_signal(barrier, inc=1, device_id=(slab, peer), device_id_type=MESH)
    for side in (up, down):
        pl.semaphore_signal(barrier, inc=1, device_id=(side, tile), device_id_type=MESH)

    loads = []
    for n, (source, target) in enumerate(((particles, pbuf), (dest_in, dest), (nbr_in, nbr), (cnt_in, cnt))):
        loads.append(pltpu.make_async_copy(source, target, in_sem.at[n]))
        loads[-1].start()

    zeros = jnp.zeros((CELL, LANES), F32)
    ones = jnp.ones((CELL, LANES), F32)
    depth = lax.broadcasted_iota(jnp.int32, (CELL, LANES), 0)

    def spread(ref, row):
        return (row // CELL) * (ref.shape[0] // 4)

    def constants():
        late = jnp.where(depth >= 4, 1.0, 0.0)
        early = jnp.where(depth < 2, 1.0, 0.0)
        middle = jnp.where((depth >= 2) & (depth < 5), 1.0, 0.0)
        fills = ((self_rows, slots, {1: late, 2: early, 3: zeros}),)
        fills += ((cand_d, 3 * slots, {1: late, 2: zeros, 3: zeros}),)
        fills += ((cand_s, 3 * slots, {0: zeros, 1: zeros, 2: middle, 3: zeros}),)
        fills += ((force_rows, 3 * slots, {1: zeros, 3: zeros}),)
        for ref, count, blocks in fills:

            @pl.loop(0, count // 8)
            def _(i):
                for r in range(8):
                    for kb, value in blocks.items():
                        ref[pl.ds(pl.multiple_of((kb * count + 8 * i + r) * CELL, CELL), CELL), :] = value

    loads[0].wait()
    loads[1].wait()

    cell = lax.broadcasted_iota(jnp.int32, (slots, bins), 0)
    hot = (cell == dest[...]).astype(BF16)
    hot = jnp.concatenate([hot, hot, hot], axis=1)

    def pack(lo, hi):
        for at in range(lo, hi):
            field = pbuf[pl.ds(ORDER[at], bins, stride=FIELDS), :]
            parts = jnp.concatenate([p.astype(BF16) for p in halves(field, 3)], axis=0)
            outbox[at] = jnp.dot(hot, parts, preferred_element_type=F32)

    mine = pl.ds(pl.multiple_of(tile * CELL, CELL), CELL)
    own_mine = pl.ds(pl.multiple_of(slots + tile * CELL, CELL), CELL)

    def landing(group, rows, own_rows):
        if group == 0:
            return pool1.at[:, own_rows, :]
        if group == 1:
            return pool2.at[:, own_rows, :]
        return carried.at[:, rows, :]

    def send(group):
        lo, hi = GROUPS[group]
        copies = []
        for i in sorted(range(1, n_tile), key=lambda j: min(j, n_tile - j)):
            peer = lax.rem(tile + i, n_tile)
            theirs = pl.ds(pl.multiple_of(peer * CELL, CELL), CELL)
            copy = pltpu.make_async_remote_copy(
                src_ref=outbox.at[lo:hi, theirs, :],
                dst_ref=landing(group, mine, own_mine),
                send_sem=a2a_send.at[group, i],
                recv_sem=a2a_recv.at[group, i],
                device_id=(slab, peer),
                device_id_type=MESH,
            )
            copy.start()
            copies.append((i, copy))
        pltpu.make_async_copy(
            outbox.at[lo:hi, mine, :], landing(group, mine, own_mine), a2a_recv.at[group, 0]
        ).start()
        return copies

    def settle(group):
        lo, hi = GROUPS[group]
        pltpu.make_async_copy(
            outbox.at[lo:hi, mine, :], landing(group, mine, own_mine), a2a_recv.at[group, 0]
        ).wait()

    def forward(kind, i):
        pool, fields = ((pool1, 5), (pool2, 3))[kind]
        source = lax.rem(tile + n_tile - i, n_tile) if i else tile
        copies = []
        for side, (target, base) in enumerate(((up, 0), (down, 2 * slots))):
            copy = pltpu.make_async_remote_copy(
                src_ref=pool.at[0:fields, pl.ds(pl.multiple_of(slots + source * CELL, CELL), CELL), :],
                dst_ref=pool.at[0:fields, pl.ds(pl.multiple_of(base + source * CELL, CELL), CELL), :],
                send_sem=halo_send.at[kind, side, i],
                recv_sem=halo_recv.at[kind, side, i],
                device_id=(target, tile),
                device_id_type=MESH,
            )
            copy.start()
            copies.append(copy)
        return copies

    def prepare(g, own):
        at = pl.ds(pl.multiple_of(g * CELL, CELL), CELL)
        mass = pool1[3, at, :]
        width = jnp.where(mass > 0, pool1[4, at, :], 1.0)
        masses[at, :] = mass
        q1, q2 = halves(0.25 * width, 2)
        q = q1 + q2
        norm = jnp.zeros((CELL, LANES), F32)

        def put(ref, row, value, group):
            ref[pl.ds(spread(ref, row) + group * CELL * CELL + row % CELL, CELL, stride=CELL), :] = value

        go = g - groups
        for d in range(3):
            x1, x2 = halves(pool1[d, at, :] - 1.0, 2)
            x = x1 + x2
            xs[d, at, :] = x
            norm = norm + x * x
            for r, (a, c) in enumerate(((x1, x1), (x1, x2), (x2, x1), (x2, x2))):
                put(cand_d, 4 * d + r, -2.0 * c, g)
                if own:
                    put(self_rows, 4 * d + r, a, go)
        for r, n in enumerate(halves(norm, 3)):
            put(cand_d, 15 + r, n, g)
            if own:
                put(self_rows, 12 + r, n, go)
        for r, n in enumerate(halves(q * q, 3)):
            put(cand_s, 15 + r, n, g)
            if own:
                put(self_rows, 18 + r, n, go)
        for r, (a, c) in enumerate(((q1, q1), (q1, q2), (q2, q1), (q2, q2))):
            put(cand_s, 21 + r, 2.0 * c, g)
            if own:
                put(self_rows, 21 + r, a, go)

    def slot_rows(ref, j):
        count = ref.shape[0] // 4
        return jnp.concatenate([ref[pl.ds(kb * count + j * CELL, CELL), :] for kb in range(4)], axis=0)

    def tile_rows(ref, j):
        return slot_rows(ref, j).astype(BF16)

    lane = lax.broadcasted_iota(jnp.int32, (ROWS, LANES), 1)

    def measure(buffer, t, block, r, j):
        far = jnp.concatenate([tile_rows(cand_d, j), tile_rows(cand_s, j)], axis=1)
        parts = [far]
        if r > 0:
            parts.insert(0, jnp.zeros((r * ROWS, 2 * LANES), BF16))
        if r < 3:
            parts.append(jnp.zeros(((3 - r) * ROWS, 2 * LANES), BF16))
        buffer[t] = jnp.dot(turned[block], jnp.concatenate(parts, axis=0), preferred_element_type=F32)

    def weigh(buffer, i, tiles):
        for at in range(0, LANES, ROWS):
            rows = slice(at, at + ROWS)
            w = None
            for t, place, mass in tiles:
                square = jnp.maximum(buffer[t, rows, 0:LANES], 1e-12)
                inv = lax.rsqrt(buffer[t, rows, LANES:])
                e = jnp.maximum(4.0 - (square * lax.rsqrt(square)) * inv, 0.0)
                h = e * inv
                g = (h * h) * h
                slope = g * (inv * inv)
                slopes[place, rows, :] = slope
                term = (g * (e * (5.0 - e))) * mass
                w = term if w is None else w + term
            column = jnp.sum(w, axis=1, keepdims=True)
            columns[rows, :] += jnp.where(lane == i, column, 0.0)

    def used(i, k):
        return lax.min(lax.max(cnt[i] - k, 0), 1).astype(F32)

    def offset_of(n):
        odd = lax.rem(n, 2)
        return odd * lax.div(n + 1, 2) + (1 - odd) * lax.rem(n_tile - lax.div(n, 2), n_tile)

    def source_of(n):
        return lax.rem(tile + n_tile - offset_of(n), n_tile)

    def self_measure(buffer, b):
        for r in range(4):
            measure(buffer, r, b, r, slots + 4 * b + r)

    def self_weigh(buffer, b):
        for r in range(4):
            i = 4 * b + r
            weigh(buffer, i, [(r, 4 * i, masses[slots + i][None, :])])

    def against_self(lo, hi):
        @pl.loop(lo, hi)
        def _(n):
            source = source_of(n)
            prepare(source + groups, True)

        for n in range(lo, hi):
            for h in range(2):
                b = 2 * source_of(jnp.int32(n)) + h
                rows = [slot_rows(self_rows, 4 * b + r) for r in range(4)]
                turned[b] = jnp.concatenate(rows, axis=0).T.astype(BF16)

        self_measure(even, 2 * source_of(jnp.int32(lo)))

        @pl.loop(lo, hi)
        def _(n):
            b = 2 * source_of(n)
            self_measure(odd, b + 1)
            self_weigh(even, b)
            self_measure(even, 2 * source_of(lax.min(n + 1, hi - 1)))
            self_weigh(odd, b + 1)

    pack(*GROUPS[0])
    pl.semaphore_wait(barrier, n_tile + 1)
    waiting = send(0)
    by_offset = dict(waiting)
    columns[...] = jnp.zeros((LANES, LANES), F32)
    constants()
    pack(*GROUPS[1])
    pack(*GROUPS[2])
    settle(0)
    forwarded = [forward(0, 0)]
    second = []
    cuts = sorted({min(c, n_tile) for c in (0, 3, 5, 8)} | {n_tile})
    for lo, hi in zip(cuts[:-1], cuts[1:]):
        for n in range(max(lo, 1), hi):
            i = (n + 1) // 2 if n % 2 else n_tile - n // 2
            by_offset[i].wait_recv()
            forwarded.append(forward(0, i))
        if hi == n_tile:
            second = send(1)
        against_self(lo, hi)

    for copies in forwarded:
        for copy in copies:
            copy.wait_recv()

    @pl.loop(0, groups)
    def _(g):
        prepare(g, False)
        prepare(g + 2 * groups, False)

    for load in loads[2:]:
        load.wait()

    chunk = slots // 2

    def others_measure(buffer, b, r):
        for k in range(1, 4):
            measure(buffer, k - 1, b, r, nbr[k, 4 * b + r])

    def others_weigh(buffer, b, r):
        i = 4 * b + r
        tiles = []
        for k in range(1, 4):
            tiles.append((k - 1, 4 * i + k, masses[nbr[k, i]][None, :] * used(i, k)))
        weigh(buffer, i, tiles)

    def ratio_copies(c):
        rows = c * chunk
        return [
            pltpu.make_async_remote_copy(
                src_ref=poolr.at[pl.ds(slots + rows, chunk), :],
                dst_ref=poolr.at[pl.ds(base + rows, chunk), :],
                send_sem=r_send.at[side, c],
                recv_sem=r_recv.at[side, c],
                device_id=(target, tile),
                device_id_type=MESH,
            )
            for side, (target, base) in enumerate(((up, 0), (down, 2 * slots)))
        ]

    others_measure(even, 0, 0)
    for c in range(2):
        @pl.loop(0, chunk // 4)
        def _(p):
            b = c * (chunk // 4) + p
            for r in range(4):
                ahead, now = (odd, even) if r % 2 == 0 else (even, odd)
                if r < 3:
                    others_measure(ahead, b, r + 1)
                else:
                    others_measure(ahead, lax.min(b + 1, slots // 4 - 1), 0)
                others_weigh(now, b, r)

        if c == 0:
            settle(1)
            for _, copy in second:
                copy.wait_recv()
            passed = [forward(1, i) for i in range(n_tile)]
            third = send(2)

        rho[...] = columns[...].T * W_SCALE

        @pl.loop(0, chunk // CELL)
        def _(p):
            row = pl.multiple_of(c * chunk + p * CELL, CELL)
            at = pl.ds(slots + row, CELL)
            density = rho[pl.ds(row, CELL), :]
            pressure = (ADIABATIC - 1.0) * density * pool2[3, at, :]
            safe = jnp.where(pool1[3, at, :] > 0, density, 1.0)
            poolr[at, :] = pressure / (safe * safe)

        for copy in ratio_copies(c):
            copy.start()

    r_copies = ratio_copies(0) + ratio_copies(1)

    for copies in passed:
        for copy in copies:
            copy.wait_recv()

    def put_force(row, g, value):
        high, low = halves(value, 2)
        for base, part in ((row, high), (row + 16, low)):
            at = pl.ds(spread(force_rows, base) + g * CELL * CELL + base % CELL, CELL, stride=CELL)
            force_rows[at, :] = part

    def prepare_motion(g):
        at = pl.ds(pl.multiple_of(g * CELL, CELL), CELL)
        mass = pool1[3, at, :]
        x = [xs[d, at, :] for d in range(3)]
        v = [pool2[d, at, :] for d in range(3)]
        put_force(0, g, mass)
        for d in range(3):
            put_force(1 + d, g, mass * x[d])
            put_force(8 + d, g, mass * v[d])
        put_force(11, g, mass * (x[0] * v[0] + x[1] * v[1] + x[2] * v[2]))

    def prepare_ratio(g):
        at = pl.ds(pl.multiple_of(g * CELL, CELL), CELL)
        massed = pool1[3, at, :] * poolr[at, :]
        put_force(4, g, massed)
        for d in range(3):
            put_force(5 + d, g, massed * xs[d, at, :])

    def pull(tiles):
        lefts, rights = [], []
        for j, place, weight in tiles:
            rows = (slot_rows(force_rows, j) * weight).astype(BF16)
            slope = slopes[place]
            high = slope.astype(BF16)
            lefts += [rows, rows]
            rights += [high, (slope - high.astype(F32)).astype(BF16)]
        out = lax.dot_general(
            jnp.concatenate(lefts, axis=1),
            jnp.concatenate(rights, axis=1),
            (((1,), (1,)), ((), ())),
            preferred_element_type=F32,
        )
        return out[0:16] + out[16:32]

    @pl.loop(0, groups)
    def _(g):
        prepare_motion(g + groups)
        prepare_ratio(g + groups)

    @pl.loop(0, slots // 16)
    def _(b):
        for r in range(16):
            i = 16 * b + r
            sums[pl.ds(pl.multiple_of(i * 16, 16), 16), :] = pull([(slots + i, 4 * i, 1.0)])

    @pl.loop(0, groups)
    def _(g):
        prepare_motion(g)
        prepare_motion(g + 2 * groups)

    for copy in r_copies:
        copy.wait_recv()

    @pl.loop(0, groups)
    def _(g):
        prepare_ratio(g)
        prepare_ratio(g + 2 * groups)

    @pl.loop(0, slots // 16)
    def _(b):
        for r in range(16):
            i = 16 * b + r
            tiles = [(nbr[k, i], 4 * i + k, used(i, k)) for k in range(1, 4)]
            sums[pl.ds(pl.multiple_of(i * 16, 16), 16), :] += pull(tiles)

    settle(2)
    for _, copy in third:
        copy.wait_recv()

    @pl.loop(0, groups)
    def _(g):
        at = pl.ds(pl.multiple_of(g * CELL, CELL), CELL)
        own = pl.ds(pl.multiple_of(slots + g * CELL, CELL), CELL)
        t = [sums[pl.ds(g * CELL * 16 + r, CELL, stride=16), :] * G_SCALE for r in range(12)]
        x = [xs[d, own, :] for d in range(3)]
        v = [pool2[d, own, :] for d in range(3)]
        mass = pool1[3, own, :]
        ratio = poolr[own, :]
        present = jnp.where(mass > 0, 1.0, 0.0)
        accel = [-(ratio * (x[d] * t[0] - t[1 + d]) + (x[d] * t[4] - t[5 + d])) for d in range(3)]
        heat = t[11]
        for d in range(3):
            heat = heat + x[d] * (v[d] * t[0] - t[8 + d]) - v[d] * t[1 + d]
        heat = ratio * heat
        speed = [v[d] + TIMESTEP * accel[d] for d in range(3)]
        place = [pool1[d, own, :] + TIMESTEP * speed[d] for d in range(3)]
        energy = pool2[3, own, :] + TIMESTEP * heat
        fields = place + speed + [mass, energy, pool1[4, own, :]] + [carried[f, at, :] for f in range(7)]
        for f, value in enumerate(fields):
            updated[pl.ds(g * CELL * FIELDS + f, CELL, stride=FIELDS), :] = value * present
        for f, value in enumerate([rho[at, :]] + accel + [heat]):
            derived[f, at, :] = value * present

    for copies in (waiting, second, third):
        for _, copy in copies:
            copy.wait_send()
    for copies in forwarded + passed:
        for copy in copies:
            copy.wait_send()
    for copy in r_copies:
        copy.wait_send()


def step(n_slab, n_tile, particles, dest_slot, neighbours, counts):
    slots = n_tile * CELL
    bins = particles.shape[0]
    dma = pltpu.SemaphoreType.DMA
    vmem = pl.BlockSpec(memory_space=pltpu.VMEM)
    updated, derived = pl.pallas_call(
        functools.partial(kernel, n_slab, n_tile),
        out_shape=(
            jax.ShapeDtypeStruct((slots * FIELDS, LANES), F32),
            jax.ShapeDtypeStruct((5, slots, LANES), F32),
        ),
        in_specs=[pl.BlockSpec(memory_space=pl.ANY)] * 4,
        out_specs=(vmem, vmem),
        scratch_shapes=[
            pltpu.SMEM((4, slots), jnp.int32),
            pltpu.SMEM((slots,), jnp.int32),
            pltpu.VMEM((1, bins), jnp.int32),
            pltpu.VMEM((bins * FIELDS, LANES), F32),
            pltpu.VMEM((FIELDS, slots, LANES), F32),
            pltpu.VMEM((5, 3 * slots, LANES), F32),
            pltpu.VMEM((4, 3 * slots, LANES), F32),
            pltpu.VMEM((7, slots, LANES), F32),
            pltpu.VMEM((3 * slots, LANES), F32),
            pltpu.VMEM((3, 3 * slots, LANES), F32),
            pltpu.VMEM((slots * ROWS, LANES), F32),
            pltpu.VMEM((3 * slots * ROWS, LANES), F32),
            pltpu.VMEM((3 * slots * ROWS, LANES), F32),
            pltpu.VMEM((3 * slots * ROWS, LANES), F32),
            pltpu.VMEM((slots * 4, LANES, LANES), F32),
            pltpu.VMEM((LANES, LANES), F32),
            pltpu.VMEM((slots * 16, LANES), F32),
            pltpu.VMEM((3 * slots, LANES), F32),
            pltpu.VMEM((slots // 4, LANES, LANES), BF16),
            pltpu.VMEM((4, LANES, 2 * LANES), F32),
            pltpu.VMEM((4, LANES, 2 * LANES), F32),
            pltpu.VMEM((LANES, LANES), F32),
            dma((4,)),
            dma((3, n_tile)),
            dma((3, n_tile)),
            dma((2, 2, n_tile)),
            dma((2, 2, n_tile)),
            dma((2, 2)),
            dma((2, 2)),
        ],
        compiler_params=pltpu.CompilerParams(collective_id=0, has_side_effects=True, vmem_limit_bytes=VMEM_BYTES),
    )(*(
        pltpu.with_memory_space_constraint(x, pltpu.HBM)
        for x in (neighbours.T, counts, dest_slot.reshape(1, bins), particles.reshape(bins * FIELDS, LANES))
    ))
    return updated.reshape(slots, FIELDS, LANES), derived.transpose(1, 0, 2)


def solution(mesh):
    in_specs = (
        P(("slab", "tile"), None, None),
        P(("slab", "tile")),
        P(("slab", "tile"), None),
        P(("slab", "tile")),
    )
    out_specs = (P(("slab", "tile"), None, None), P(("slab", "tile"), None, None))
    body = functools.partial(step, mesh.shape["slab"], mesh.shape["tile"])
    return jax.shard_map(body, mesh=mesh, in_specs=in_specs, out_specs=out_specs, check_vma=False)
```
